128 devices in a mesh: pipe: 8 (over x, y_lo), dp: 16 (over y_hi, z, core).
Axes of the slice: x: 4, y: 4 (y_hi: 2, y_lo: 2; y = y_hi * 2 + y_lo), z: 4, core: 2. Of those that a mesh axis runs over, the one named last changes fastest.
Arguments:
- inputs: bfloat16 [6, 512, 8192], P(None, 'dp'), may hold values from -6 to 6
- cotangent: bfloat16 [6, 512, 8192], P(None, 'dp'), may hold values from -0.19921875 to 0.19921875
- plan_order: int32 [6], replicated, may hold values from 0 to 5, each once
- norm_gain: float32 [8, 8192], P('pipe'), may hold values from 0.5 to 1.5
- weight_in: bfloat16 [8, 8192, 512], P('pipe'), may hold values from -0.0625 to 0.0625
- weight_out: bfloat16 [8, 512, 8192], P('pipe'), may hold values from -0.25 to 0.25
Outputs:
- grad_in: bfloat16 [8, 8192, 512], P('pipe', 'dp')
- grad_out: bfloat16 [8, 512, 8192], P('pipe', None, 'dp')
The draws below stay inside these ranges and needn't reach their ends.
Inputs may be any that keep to these rules, and one draw needn't show every extreme that they name: plan_order names each slot's sample once: a permutation.
All inputs are finite; a program needn't handle non-finite values.
Results may differ from the reference program's by a relative error of at most 0.024.
Values may be sent and summed in bfloat16 or wider, within the bound.
No kernel may reach another device: no remote copies, remote signals or barrier semaphores. Data moves between devices by JAX's collectives and lax.ppermute only.
A program may use at most 128 MiB of HBM per device.

```python
import jax
import jax.numpy as jnp
from jax import lax

D = 8192
R = 512
MICRO = 6
ROWS = 512
SECTIONS = 8
N_DP = 16


def raised(entries, own_key, source, target, parts, factor):
    def block_of(position):
        return (jnp.arange(entries.shape[position]) // (entries.shape[position] // parts)).reshape((-1,) + (1,) * (entries.ndim - 1 - position))

    near = jax.random.permutation(own_key, parts)[block_of(target)]
    far = (block_of(target) + parts // 2) % parts
    return jnp.where((block_of(source) == near) | (block_of(source) == far), factor * entries, entries)


def level_of(key, dims, cuts, low, top_value):
    gain = 1.0
    for dim, blocks in cuts:
        draws = jax.random.uniform(jax.random.fold_in(jax.random.fold_in(key, 6), dim), (blocks,), jnp.float32, low / len(cuts), top_value / len(cuts))
        gain = gain * jnp.repeat(jnp.exp(draws), dims[dim] // blocks).reshape((-1,) + (1,) * (len(dims) - 1 - dim))
    return gain


def bell_draw(key, dims, deviation, most, cuts=(), kind=jnp.bfloat16):
    factor_of = level_of(key, dims, cuts, -0.22, 0.18) if cuts else 1.0
    entries = jax.random.normal(key, dims, jnp.float32) * deviation * factor_of
    return jnp.minimum(jnp.maximum(entries, -most), most).astype(kind)


def bell_draw_with(own_key, shape, deviation, reach, cuts, heavy, held_as=jnp.bfloat16):
    values = deviation * jax.random.normal(own_key, shape, jnp.float32)
    if cuts:
        values = values * level_of(own_key, shape, cuts, -0.22, 0.18)
    return jnp.clip(raised(values, jax.random.fold_in(own_key, 3), *heavy), -reach, reach).astype(held_as)


def setup_inputs(seed: int = 0) -> dict:
    keys = jax.random.split(jax.random.key(seed), 7)
    return {
        "inputs": bell_draw_with(keys[0], (MICRO, ROWS, D), 1.0, 6.0, ((1, 16),), (1, 2, 16, 2.0)),
        "cotangent": bell_draw_with(keys[1], (MICRO, ROWS, D), 0.03, 0.19921875, ((1, 16),), (1, 2, 16, 2.0)),
        "plan_order": jax.random.permutation(keys[2], MICRO).astype(jnp.int32),
        "norm_gain": jnp.clip(1.0 + 0.1 * jax.random.normal(keys[3], (SECTIONS, D), jnp.float32), 0.5, 1.5),
        "weight_in": bell_draw(keys[4], (SECTIONS, D, R), D ** -0.5, 0.0625, ((0, 8),)),
        "weight_out": bell_draw(keys[5], (SECTIONS, R, D), R ** -0.5, 0.25, ((0, 8),)),
    }


EPSILON = 1e-05

def inner_section(rows_in, gain_row, weight_first):
    float_cast = rows_in.astype(jnp.float32)
    inverse_root_mean = lax.rsqrt(lax.optimization_barrier(jnp.mean(float_cast * float_cast, axis=-1, keepdims=True)) + EPSILON)
    normed = (float_cast * inverse_root_mean * gain_row).astype(jnp.bfloat16)
    pre_act = jnp.dot(normed, weight_first, preferred_element_type=jnp.float32)
    hidden = jax.nn.silu(pre_act).astype(jnp.bfloat16)
    return (float_cast, inverse_root_mean, normed, pre_act, hidden)

def reference(inputs, cotangent, plan_order, norm_gain, weight_in, weight_out):
    section_count = norm_gain.shape[0]
    micro_count, row_count, model_width = inputs.shape
    inner_width = weight_in.shape[2]
    rows_now = inputs[plan_order.astype(jnp.int32)].reshape(micro_count * row_count, model_width)
    saved = []
    for section_index in range(section_count):
        saved.append(rows_now)
        float_cast, inverse_root_mean, normed, pre_act, hidden = inner_section(rows_now, norm_gain[section_index], weight_in[section_index])
        rows_now = (float_cast + jnp.dot(hidden, weight_out[section_index], preferred_element_type=jnp.float32)).astype(jnp.bfloat16)

    def split_dp(array):
        last = array.shape[-1]
        grouped = array.reshape(micro_count, N_DP, row_count // N_DP, last)
        return jnp.transpose(grouped, (1, 0, 2, 3)).reshape(N_DP, -1, last)

    def add_source(totals, items):
        normed_q, grad_q, hidden_q, up_q = items
        term_in = jnp.dot(normed_q.T, grad_q, preferred_element_type=jnp.float32)
        term_out = jnp.dot(hidden_q.T, up_q, preferred_element_type=jnp.float32)
        term_in = lax.optimization_barrier(term_in.astype(jnp.bfloat16)).astype(jnp.float32)
        term_out = lax.optimization_barrier(term_out.astype(jnp.bfloat16)).astype(jnp.float32)
        return ((totals[0] + term_in, totals[1] + term_out), None)
    incoming_gradient = cotangent.reshape(micro_count * row_count, model_width)
    grads_first = [None] * section_count
    grads_second = [None] * section_count
    for section_index in reversed(range(section_count)):
        gain_row = norm_gain[section_index]
        float_cast, inverse_root_mean, normed, pre_act, hidden = inner_section(saved[section_index], gain_row, weight_in[section_index])
        grad_hidden = jnp.dot(incoming_gradient, weight_out[section_index].T, preferred_element_type=jnp.float32)
        sigmoid_pre = jax.nn.sigmoid(pre_act)
        grad_pre = (grad_hidden * sigmoid_pre * (1.0 + pre_act * (1.0 - sigmoid_pre))).astype(jnp.bfloat16)
        back_rows = jnp.dot(grad_pre, weight_in[section_index].T, preferred_element_type=jnp.float32)
        zeros_in = jnp.zeros((model_width, inner_width), jnp.float32)
        zeros_out = jnp.zeros((inner_width, model_width), jnp.float32)
        (total_in, total_out), unused = lax.scan(add_source, (zeros_in, zeros_out), (split_dp(normed), split_dp(grad_pre), split_dp(hidden), split_dp(incoming_gradient)))
        grads_first[section_index] = total_in.astype(jnp.bfloat16)
        grads_second[section_index] = total_out.astype(jnp.bfloat16)
        normalized_input = float_cast * inverse_root_mean
        rescaled_rows = back_rows * gain_row
        incoming_gradient = (incoming_gradient.astype(jnp.float32) + inverse_root_mean * (rescaled_rows - normalized_input * lax.optimization_barrier(jnp.mean(rescaled_rows * normalized_input, axis=-1, keepdims=True)))).astype(jnp.bfloat16)
    return (jnp.stack(grads_first), jnp.stack(grads_second))
```

```python
import functools

import jax
import jax.numpy as jnp
from jax import lax
from jax.experimental import pallas as pl
from jax.experimental.pallas import tpu as pltpu
from jax.sharding import PartitionSpec as P

EPSILON = 1e-05
SPLIT = 2
SKEW = 2
AUX = 128
CUT = 1024

F32 = jnp.float32
BF16 = jnp.bfloat16


def hbm():
    return pl.BlockSpec(memory_space=pl.ANY)


def vmem():
    return pl.BlockSpec(memory_space=pltpu.VMEM)


def smem():
    return pl.BlockSpec(memory_space=pltpu.SMEM)


def load_kernel(*refs):
    count = (len(refs) - 1) // 2
    sems = refs[-1]
    copies = [
        pltpu.make_async_copy(refs[k], refs[count + k], sems.at[k]) for k in range(count)
    ]
    for copy in copies:
        copy.start()
    for copy in copies:
        copy.wait()


def resident(*arrays):
    return pl.pallas_call(
        load_kernel,
        out_shape=tuple(pltpu.VMEM(a.shape, a.dtype) for a in arrays),
        in_specs=[hbm()] * len(arrays),
        out_specs=tuple(vmem() for a in arrays),
        scratch_shapes=[pltpu.SemaphoreType.DMA((len(arrays),))],
        compiler_params=pltpu.CompilerParams(vmem_limit_bytes=1 << 20),
        name="resident",
    )(*arrays)


def fetch(take, source, other, target, sem):
    @pl.when(take)
    def _():
        copy = pltpu.make_async_copy(source, target, sem)
        copy.start()
        copy.wait()

    @pl.when(jnp.logical_not(take))
    def _():
        copy = pltpu.make_async_copy(other, target, sem)
        copy.start()
        copy.wait()


def forward_kernel(chunk, slot, meta, plan, arrived, inputs, gain, w_in, w_out, *rest):
    if slot > 0:
        rest = rest[3:]
    send, normed_all, aux_all, hidden_all, x, normed, aux, hidden, sems = rest
    rows, width = x.shape
    inner = w_in.shape[1]
    if chunk is None:
        copy = pltpu.make_async_copy(arrived, x, sems.at[0])
        copy.start()
        copy.wait()
    else:
        block, part = divmod(chunk, SPLIT)
        fresh = inputs.at[plan[block], pl.ds(part * rows, rows), :]
        fetch(meta[0] == 0, fresh, arrived, x, sems.at[0])
    total = jnp.zeros((rows, CUT), F32)
    for j in range(width // CUT):
        value = x[:, j * CUT : (j + 1) * CUT].astype(F32)
        total = total + value * value
    inverse = lax.rsqrt(jnp.sum(total, axis=1, keepdims=True) / width + EPSILON)
    pre = jnp.zeros((rows, inner), F32)
    for j in range(width // CUT):
        cols = slice(j * CUT, (j + 1) * CUT)
        piece = (x[:, cols].astype(F32) * inverse * gain[:, cols]).astype(BF16)
        normed[:, cols] = piece
        pre = pre + jnp.dot(piece, w_in[cols, :], preferred_element_type=F32)
    at = pl.ds(slot * rows, rows)
    first = pltpu.make_async_copy(normed, normed_all.at[at, :], sems.at[1])
    first.start()
    aux[:, :inner] = pre
    aux[:, inner:] = jnp.broadcast_to(inverse, (rows, AUX))
    second = pltpu.make_async_copy(aux, aux_all.at[at, :], sems.at[2])
    second.start()
    act = (pre / (1.0 + jnp.exp(-pre))).astype(BF16)
    hidden[...] = act
    third = pltpu.make_async_copy(hidden, hidden_all.at[at, :], sems.at[3])
    third.start()
    for j in range(width // CUT):
        cols = slice(j * CUT, (j + 1) * CUT)
        delta = jnp.dot(act, w_out[:, cols], preferred_element_type=F32)
        send[:, cols] = (x[:, cols].astype(F32) + delta).astype(BF16)
    first.wait()
    second.wait()
    third.wait()


def forward_step(slot, ticks, chunks, rows, meta, plan, arrived, inputs, gain, w_in, w_out, kept):
    width, inner = w_in.shape
    chunk = slot if slot < chunks else None
    shapes = (
        jax.ShapeDtypeStruct((rows, width), BF16),
        jax.ShapeDtypeStruct((ticks * rows, width), BF16),
        jax.ShapeDtypeStruct((ticks * rows, inner + AUX), F32),
        jax.ShapeDtypeStruct((ticks * rows, inner), BF16),
    )
    specs = [smem(), smem(), hbm(), hbm(), vmem(), vmem(), vmem()] + [hbm()] * len(kept)
    return pl.pallas_call(
        functools.partial(forward_kernel, chunk, slot),
        out_shape=shapes,
        in_specs=specs,
        out_specs=(vmem(), hbm(), hbm(), hbm()),
        scratch_shapes=[
            pltpu.VMEM((rows, width), BF16),
            pltpu.VMEM((rows, width), BF16),
            pltpu.VMEM((rows, inner + AUX), F32),
            pltpu.VMEM((rows, inner), BF16),
            pltpu.SemaphoreType.DMA((4,)),
        ],
        input_output_aliases={7 + k: 1 + k for k in range(len(kept))},
        compiler_params=pltpu.CompilerParams(vmem_limit_bytes=8 << 20),
        cost_estimate=pl.CostEstimate(
            flops=4 * rows * width * inner, bytes_accessed=10 << 20, transcendentals=0
        ),
        name="forward_step",
    )(meta, plan, arrived, inputs, gain, w_in, w_out, *kept)


NT = (((1,), (1,)), ((), ()))


def backward_kernel(
    chunk, slot, meta, arrived, cotangent, normed_all, aux_all, gain, w_in, w_out, *rest
):
    if slot > 0:
        rest = rest[2:]
    send, up_all, grad_all, up, normed, aux, grad, sems = rest
    rows, width = up.shape
    inner = w_in.shape[1]
    source = pl.ds(pl.multiple_of(meta[1] * rows, rows), rows)
    load_normed = pltpu.make_async_copy(normed_all.at[source, :], normed, sems.at[1])
    load_normed.start()
    load_aux = pltpu.make_async_copy(aux_all.at[source, :], aux, sems.at[2])
    load_aux.start()
    if chunk is None:
        copy = pltpu.make_async_copy(arrived, up, sems.at[0])
        copy.start()
        copy.wait()
    else:
        block, part = divmod(chunk, SPLIT)
        fresh = cotangent.at[block, pl.ds(part * rows, rows), :]
        fetch(meta[0] == 1, fresh, arrived, up, sems.at[0])
    at = pl.ds(slot * rows, rows)
    store_up = pltpu.make_async_copy(up, up_all.at[at, :], sems.at[3])
    store_up.start()
    grad_hidden = jnp.zeros((rows, inner), F32)
    for j in range(width // CUT):
        cols = slice(j * CUT, (j + 1) * CUT)
        grad_hidden = grad_hidden + lax.dot_general(
            up[:, cols], w_out[:, cols], NT, preferred_element_type=F32
        )
    load_aux.wait()
    pre = aux[:, :inner]
    inverse = aux[:, inner : inner + 1]
    gate = 1.0 / (1.0 + jnp.exp(-pre))
    grad_pre = (grad_hidden * gate * (1.0 + pre * (1.0 - gate))).astype(BF16)
    grad[...] = grad_pre
    store_grad = pltpu.make_async_copy(grad, grad_all.at[at, :], sems.at[4])
    store_grad.start()
    mean = jnp.sum(grad_pre.astype(F32) * pre, axis=1, keepdims=True) / width
    load_normed.wait()
    for j in range(width // CUT):
        cols = slice(j * CUT, (j + 1) * CUT)
        back = lax.dot_general(grad_pre, w_in[cols, :], NT, preferred_element_type=F32)
        scale = gain[:, cols]
        xhat = normed[:, cols].astype(F32) * (1.0 / scale)
        send[:, cols] = (
            up[:, cols].astype(F32) + inverse * (back * scale - xhat * mean)
        ).astype(BF16)
    store_up.wait()
    store_grad.wait()


def backward_step(
    slot, ticks, chunks, rows, meta, arrived, cotangent, normed_all, aux_all, gain, w_in, w_out, kept
):
    width, inner = w_in.shape
    chunk = slot if slot < chunks else None
    shapes = (
        jax.ShapeDtypeStruct((rows, width), BF16),
        jax.ShapeDtypeStruct((ticks * rows, width), BF16),
        jax.ShapeDtypeStruct((ticks * rows, inner), BF16),
    )
    specs = [smem()] + [hbm()] * 4 + [vmem()] * 3 + [hbm()] * len(kept)
    return pl.pallas_call(
        functools.partial(backward_kernel, chunk, slot),
        out_shape=shapes,
        in_specs=specs,
        out_specs=(vmem(), hbm(), hbm()),
        scratch_shapes=[
            pltpu.VMEM((rows, width), BF16),
            pltpu.VMEM((rows, width), BF16),
            pltpu.VMEM((rows, inner + AUX), F32),
            pltpu.VMEM((rows, inner), BF16),
            pltpu.SemaphoreType.DMA((5,)),
        ],
        input_output_aliases={8 + k: 1 + k for k in range(len(kept))},
        compiler_params=pltpu.CompilerParams(vmem_limit_bytes=8 << 20),
        cost_estimate=pl.CostEstimate(
            flops=4 * rows * width * inner, bytes_accessed=10 << 20, transcendentals=0
        ),
        name="backward_step",
    )(meta, arrived, cotangent, normed_all, aux_all, gain, w_in, w_out, *kept)


def gathered(array, axis):
    return lax.all_gather(array, axis, axis=0, tiled=True)


def columns(array, axis):
    return lax.all_to_all(array, axis, split_axis=1, concat_axis=0, tiled=True)


def contracted(left, right):
    return lax.dot_general(left, right, (((0,), (0,)), ((), ())), preferred_element_type=F32)


def per_device(inputs, cotangent, plan_order, norm_gain, weight_in, weight_out):
    sections = lax.axis_size("pipe")
    section = lax.axis_index("pipe")
    micro_count, row_count, width = inputs.shape
    rows = row_count // SPLIT
    chunks = micro_count * SPLIT
    last = SKEW * (sections - 1)
    ticks = chunks + last

    def held(tick):
        return [s for s in range(sections) if 0 <= tick - SKEW * s < chunks]

    w_in, w_out = resident(weight_in[0], weight_out[0])
    empty = jnp.zeros((rows, width), BF16)
    plan = plan_order.astype(jnp.int32)

    meta = jnp.stack([section, section]).astype(jnp.int32)
    moving = {}
    kept = ()
    for tick in range(ticks):
        arrived = moving.pop(tick, empty)
        send, *kept = forward_step(
            tick, ticks, chunks, rows, meta, plan, arrived, inputs, norm_gain, w_in, w_out, kept
        )
        pairs = [(s, s + 1) for s in held(tick) if s + 1 < sections]
        if pairs:
            moving[tick + SKEW] = lax.ppermute(send, "pipe", pairs)
    normed_all, aux_all, hidden_all = kept
    tokens = chunks * rows
    half = tokens // 2
    begin = section * (SKEW * rows)
    normed_own = lax.dynamic_slice(normed_all, (begin, 0), (tokens, width))
    hidden_own = lax.dynamic_slice(hidden_all, (begin, 0), (tokens, hidden_all.shape[1]))
    normed_cols = columns(normed_own, "dp")
    hidden_rows = gathered(hidden_own, "dp")

    moving = {}
    kept = ()
    is_last = (section == sections - 1).astype(jnp.int32)
    for tick in range(ticks):
        arrived = moving.pop(tick, empty)
        source = jnp.clip(tick - last + 2 * SKEW * section, 0, ticks - 1).astype(jnp.int32)
        send, *kept = backward_step(
            tick,
            ticks,
            chunks,
            rows,
            jnp.stack([is_last, source]),
            arrived,
            cotangent,
            normed_all,
            aux_all,
            norm_gain,
            w_in,
            w_out,
            kept,
        )
        pairs = [
            (sections - 1 - s, sections - 2 - s) for s in held(tick) if s + 1 < sections
        ]
        if pairs:
            moving[tick + SKEW] = lax.ppermute(send, "pipe", pairs)
    up_all, grad_all = kept
    begin = (sections - 1 - section) * (SKEW * rows)
    up_own = lax.dynamic_slice(up_all, (begin, 0), (tokens, width))
    grad_own = lax.dynamic_slice(grad_all, (begin, 0), (tokens, grad_all.shape[1]))
    up_cols = columns(up_own, "dp")
    grad_rows = gathered(grad_own, "dp")
    total_in = contracted(normed_cols, grad_rows).astype(BF16)
    total_out = contracted(hidden_rows, up_cols).astype(BF16)
    return total_in[None], total_out[None]


def solution(mesh):
    in_specs = (
        P(None, "dp", None),
        P(None, "dp", None),
        P(),
        P("pipe", None),
        P("pipe", None, None),
        P("pipe", None, None),
    )
    out_specs = (P("pipe", "dp", None), P("pipe", None, "dp"))
    return jax.shard_map(
        per_device, mesh=mesh, in_specs=in_specs, out_specs=out_specs, check_vma=False
    )
```

```python
import functools

import jax
import jax.numpy as jnp
from jax import lax
from jax.experimental import pallas as pl
from jax.experimental.pallas import tpu as pltpu
from jax.sharding import PartitionSpec as P

EPSILON = 1e-05
SPLIT = 2
SKEW = 2
AUX = 128
TOGETHER = 2

F32 = jnp.float32
BF16 = jnp.bfloat16


def hbm():
    return pl.BlockSpec(memory_space=pltpu.HBM)


def vmem():
    return pl.BlockSpec(memory_space=pltpu.VMEM)


def smem():
    return pl.BlockSpec(memory_space=pltpu.SMEM)


def across(count, body, start):
    def step(j, carry):
        for k in range(TOGETHER):
            carry = body(j * TOGETHER + k, carry)
        return carry

    return lax.fori_loop(0, count // TOGETHER, step, start)


def kept_in(space, *arrays):
    return [pltpu.with_memory_space_constraint(a, space) for a in arrays]


def load_kernel(*refs):
    count = (len(refs) - 1) // 2
    sems = refs[-1]
    copies = [
        pltpu.make_async_copy(refs[k], refs[count + k], sems.at[k]) for k in range(count)
    ]
    for copy in copies:
        copy.start()
    for copy in copies:
        copy.wait()


def resident(*arrays):
    return pl.pallas_call(
        load_kernel,
        out_shape=tuple(pltpu.VMEM(a.shape, a.dtype) for a in arrays),
        in_specs=[hbm()] * len(arrays),
        out_specs=tuple(vmem() for a in arrays),
        scratch_shapes=[pltpu.SemaphoreType.DMA((len(arrays),))],
        compiler_params=pltpu.CompilerParams(vmem_limit_bytes=1 << 20),
        name="resident",
    )(*kept_in(pltpu.HBM, *arrays))


def spread(source, target, sem):
    count, rows, cut = target.shape
    return [
        pltpu.make_async_copy(source.at[:, pl.ds(j * cut, cut)], target.at[j], sem)
        for j in range(count)
    ]


def fetch(fresh, fresh_here, arrived, target, sem):
    moved = pltpu.make_async_copy(arrived, target, sem)
    if fresh is None:
        moved.start()
        moved.wait()
        return

    @pl.when(fresh_here)
    def _():
        copies = spread(fresh, target, sem)
        for copy in copies:
            copy.start()
        moved.wait()

    @pl.when(jnp.logical_not(fresh_here))
    def _():
        moved.start()
        moved.wait()


def block(j, cut):
    return pl.ds(pl.multiple_of(j * cut, cut), cut)


def forward_kernel(tick, chunks, place, plan, arrived, inputs, gain, w_in, w_out, *rest):
    if tick > 0:
        rest = rest[3:]
    send, normed_all, aux_all, hidden_all, x, normed, aux, hidden, sems = rest
    count, rows, cut = x.shape
    width = count * cut
    inner = w_in.shape[1]
    fresh = None
    if tick < chunks:
        slot, part = divmod(tick, SPLIT)
        fresh = inputs.at[plan[slot], pl.ds(part * rows, rows), :]
    fetch(fresh, place[0] == 0, arrived, x, sems.at[0])
    mine = tick - SKEW * place[0]
    active = jnp.logical_and(mine >= 0, mine < chunks)
    at = pl.ds(pl.multiple_of(jnp.clip(mine, 0, chunks - 1) * rows, rows), rows)
    stores = [
        pltpu.make_async_copy(normed, normed_all.at[:, at, :], sems.at[1]),
        pltpu.make_async_copy(aux, aux_all.at[at, :], sems.at[2]),
        pltpu.make_async_copy(hidden, hidden_all.at[at, :], sems.at[3]),
    ]

    def squares(j, total):
        value = x[j].astype(F32)
        return total + value * value

    total = across(count, squares, jnp.zeros((rows, cut), F32))
    inverse = lax.rsqrt(jnp.sum(total, axis=1, keepdims=True) / width + EPSILON)

    def project(j, pre):
        piece = (x[j].astype(F32) * inverse * gain[:, block(j, cut)]).astype(BF16)
        normed[j] = piece
        return pre + jnp.dot(piece, w_in[block(j, cut), :], preferred_element_type=F32)

    pre = across(count, project, jnp.zeros((rows, inner), F32))
    aux[:, :inner] = pre
    aux[:, inner:] = jnp.broadcast_to(inverse, (rows, AUX))
    act = (pre / (1.0 + jnp.exp(-pre))).astype(BF16)
    hidden[...] = act

    @pl.when(active)
    def _():
        for store in stores:
            store.start()

    def expand(j, nothing):
        delta = jnp.dot(act, w_out[:, block(j, cut)], preferred_element_type=F32)
        send[j] = (x[j].astype(F32) + delta).astype(BF16)
        return nothing

    across(count, expand, 0)

    @pl.when(active)
    def _():
        for store in stores:
            store.wait()


def forward_step(tick, chunks, rows, count, place, plan, arrived, inputs, gain, w_in, w_out, kept):
    width, inner = w_in.shape
    cut = width // count
    shapes = (
        jax.ShapeDtypeStruct((count, rows, cut), BF16),
        pltpu.HBM((count, chunks * rows, cut), BF16),
        pltpu.HBM((chunks * rows, inner + AUX), F32),
        pltpu.HBM((chunks * rows, inner), BF16),
    )
    specs = [smem(), smem(), hbm(), hbm(), vmem(), vmem(), vmem()] + [hbm()] * len(kept)
    return pl.pallas_call(
        functools.partial(forward_kernel, tick, chunks),
        out_shape=shapes,
        in_specs=specs,
        out_specs=(vmem(), hbm(), hbm(), hbm()),
        scratch_shapes=[
            pltpu.VMEM((count, rows, cut), BF16),
            pltpu.VMEM((count, rows, cut), BF16),
            pltpu.VMEM((rows, inner + AUX), F32),
            pltpu.VMEM((rows, inner), BF16),
            pltpu.SemaphoreType.DMA((4,)),
        ],
        input_output_aliases={7 + k: 1 + k for k in range(len(kept))},
        compiler_params=pltpu.CompilerParams(vmem_limit_bytes=8 << 20),
        cost_estimate=pl.CostEstimate(
            flops=4 * rows * width * inner, bytes_accessed=10 << 20, transcendentals=0
        ),
        name="forward_step",
    )(
        place,
        plan,
        arrived,
        *kept_in(pltpu.HBM, inputs),
        gain,
        *kept_in(pltpu.VMEM, w_in, w_out),
        *kept_in(pltpu.HBM, *kept),
    )


def backward_kernel(
    tick, chunks, sections, place, arrived, cotangent, normed_all, aux_all, gain, w_in, w_out, *rest
):
    if tick > 0:
        rest = rest[2:]
    send, up_all, grad_all, up, normed, aux, grad, sems = rest
    count, rows, cut = up.shape
    width = count * cut
    inner = w_in.shape[0]
    mine = tick - SKEW * (sections - 1 - place[0])
    active = jnp.logical_and(mine >= 0, mine < chunks)
    at = pl.ds(pl.multiple_of(jnp.clip(mine, 0, chunks - 1) * rows, rows), rows)
    load_normed = pltpu.make_async_copy(normed_all.at[:, at, :], normed, sems.at[1])
    load_normed.start()
    load_aux = pltpu.make_async_copy(aux_all.at[at, :], aux, sems.at[2])
    load_aux.start()
    fresh = None
    if tick < chunks:
        slot, part = divmod(tick, SPLIT)
        fresh = cotangent.at[slot, pl.ds(part * rows, rows), :]
    fetch(fresh, place[0] == sections - 1, arrived, up, sems.at[0])
    store_up = pltpu.make_async_copy(up, up_all.at[:, at, :], sems.at[3])
    store_grad = pltpu.make_async_copy(grad, grad_all.at[at, :], sems.at[4])

    @pl.when(active)
    def _():
        store_up.start()

    def project(j, total):
        return total + jnp.dot(up[j], w_out[block(j, cut), :], preferred_element_type=F32)

    grad_hidden = across(count, project, jnp.zeros((rows, inner), F32))
    load_aux.wait()
    pre = aux[:, :inner]
    inverse = aux[:, inner : inner + 1]
    gate = 1.0 / (1.0 + jnp.exp(-pre))
    grad_pre = (grad_hidden * gate * (1.0 + pre * (1.0 - gate))).astype(BF16)
    grad[...] = grad_pre

    @pl.when(active)
    def _():
        store_grad.start()

    mean = jnp.sum(grad_pre.astype(F32) * pre, axis=1, keepdims=True) / width
    load_normed.wait()

    def expand(j, nothing):
        cols = block(j, cut)
        back = jnp.dot(grad_pre, w_in[:, cols], preferred_element_type=F32)
        scale = gain[:, cols]
        xhat = normed[j].astype(F32) * (1.0 / scale)
        send[j] = (up[j].astype(F32) + inverse * (back * scale - xhat * mean)).astype(BF16)
        return nothing

    across(count, expand, 0)

    @pl.when(active)
    def _():
        store_up.wait()
        store_grad.wait()


def backward_step(
    tick, chunks, rows, sections, place, arrived, cotangent, normed_all, aux_all, gain, w_in, w_out, kept
):
    inner, width = w_in.shape
    count = normed_all.shape[0]
    cut = width // count
    shapes = (
        jax.ShapeDtypeStruct((count, rows, cut), BF16),
        pltpu.HBM((count, chunks * rows, cut), BF16),
        pltpu.HBM((chunks * rows, inner), BF16),
    )
    specs = [smem()] + [hbm()] * 4 + [vmem()] * 3 + [hbm()] * len(kept)
    return pl.pallas_call(
        functools.partial(backward_kernel, tick, chunks, sections),
        out_shape=shapes,
        in_specs=specs,
        out_specs=(vmem(), hbm(), hbm()),
        scratch_shapes=[
            pltpu.VMEM((count, rows, cut), BF16),
            pltpu.VMEM((count, rows, cut), BF16),
            pltpu.VMEM((rows, inner + AUX), F32),
            pltpu.VMEM((rows, inner), BF16),
            pltpu.SemaphoreType.DMA((5,)),
        ],
        input_output_aliases={8 + k: 1 + k for k in range(len(kept))},
        compiler_params=pltpu.CompilerParams(vmem_limit_bytes=8 << 20),
        cost_estimate=pl.CostEstimate(
            flops=4 * rows * width * inner, bytes_accessed=10 << 20, transcendentals=0
        ),
        name="backward_step",
    )(
        place,
        arrived,
        *kept_in(pltpu.HBM, cotangent, normed_all, aux_all),
        gain,
        *kept_in(pltpu.VMEM, w_in, w_out),
        *kept_in(pltpu.HBM, *kept),
    )


def gathered(array, axis):
    return lax.all_gather(array, axis, axis=0, tiled=True)


def columns(array, axis):
    taken = lax.all_to_all(array, axis, split_axis=0, concat_axis=0, tiled=True)
    return taken.reshape(-1, array.shape[-1])


def contracted(left, right):
    return lax.dot_general(left, right, (((0,), (0,)), ((), ())), preferred_element_type=F32)


def per_device(inputs, cotangent, plan_order, norm_gain, weight_in, weight_out):
    sections = lax.axis_size("pipe")
    count = lax.axis_size("dp")
    micro_count, row_count, width = inputs.shape
    rows = row_count // SPLIT
    chunks = micro_count * SPLIT
    ticks = chunks + SKEW * (sections - 1)
    onward = [(s, s + 1) for s in range(sections - 1)]
    back = [(s + 1, s) for s in range(sections - 1)]
    place = lax.axis_index("pipe").astype(jnp.int32).reshape(1)
    plan = plan_order.astype(jnp.int32)
    empty = jnp.zeros((count, rows, width // count), BF16)

    w_in, w_out = resident(weight_in[0], weight_out[0])
    moving = {}
    kept = ()
    for tick in range(ticks):
        arrived = moving.pop(tick, empty)
        send, *kept = forward_step(
            tick, chunks, rows, count, place, plan, arrived, inputs, norm_gain, w_in, w_out, kept
        )
        if tick + SKEW < ticks:
            moving[tick + SKEW] = lax.ppermute(send, "pipe", onward)
    normed_all, aux_all, hidden_all = kept
    normed_cols = columns(normed_all, "dp")
    hidden_rows = gathered(hidden_all, "dp")

    w_in, w_out = resident(weight_in[0].T, weight_out[0].T)
    moving = {}
    kept = ()
    for tick in range(ticks):
        arrived = moving.pop(tick, empty)
        send, *kept = backward_step(
            tick,
            chunks,
            rows,
            sections,
            place,
            arrived,
            cotangent,
            normed_all,
            aux_all,
            norm_gain,
            w_in,
            w_out,
            kept,
        )
        if tick + SKEW < ticks:
            moving[tick + SKEW] = lax.ppermute(send, "pipe", back)
    up_all, grad_all = kept
    up_cols = columns(up_all, "dp")
    grad_rows = gathered(grad_all, "dp")
    total_in = contracted(normed_cols, grad_rows).astype(BF16)
    total_out = contracted(hidden_rows, up_cols).astype(BF16)
    return total_in[None], total_out[None]


def solution(mesh):
    in_specs = (
        P(None, "dp", None),
        P(None, "dp", None),
        P(),
        P("pipe", None),
        P("pipe", None, None),
        P("pipe", None, None),
    )
    out_specs = (P("pipe", "dp", None), P("pipe", None, "dp"))
    return jax.shard_map(
        per_device, mesh=mesh, in_specs=in_specs, out_specs=out_specs, check_vma=False
    )
```

```python
import functools

import jax
import jax.numpy as jnp
from jax import lax
from jax.experimental import pallas as pl
from jax.experimental.pallas import tpu as pltpu
from jax.sharding import PartitionSpec as P

EPSILON = 1e-05
CHUNKS = 8
SKEW = 2
AUX = 128
TOGETHER = 4

PARTS = 2
TIED = 12

F32 = jnp.float32
BF16 = jnp.bfloat16


def hbm():
    return pl.BlockSpec(memory_space=pltpu.HBM)


def vmem():
    return pl.BlockSpec(memory_space=pltpu.VMEM)


def smem():
    return pl.BlockSpec(memory_space=pltpu.SMEM)


def across(count, body, start):
    def step(j, carry):
        for k in range(TOGETHER):
            carry = body(j * TOGETHER + k, carry)
        return carry

    return lax.fori_loop(0, count // TOGETHER, step, start)


def kept_in(space, *arrays):
    return [pltpu.with_memory_space_constraint(a, space) for a in arrays]


def load_kernel(*refs):
    count = (len(refs) - 1) // 2
    sems = refs[-1]
    copies = [
        pltpu.make_async_copy(refs[k], refs[count + k], sems.at[k]) for k in range(count)
    ]
    for copy in copies:
        copy.start()
    for copy in copies:
        copy.wait()


def resident(*arrays):
    return pl.pallas_call(
        load_kernel,
        out_shape=tuple(pltpu.VMEM(a.shape, a.dtype) for a in arrays),
        in_specs=[hbm()] * len(arrays),
        out_specs=tuple(vmem() for a in arrays),
        scratch_shapes=[pltpu.SemaphoreType.DMA((len(arrays),))],
        compiler_params=pltpu.CompilerParams(vmem_limit_bytes=1 << 20),
        name="resident",
    )(*kept_in(pltpu.HBM, *arrays))


def spread(source, start, target, at, sem):
    count, _, cut = target.shape
    size = source.shape[0]
    return [
        pltpu.make_async_copy(
            source.at[:, pl.ds(j * cut, cut)], target.at[j, pl.ds(at, size), :], sem
        )
        for j in range(count)
    ]


def pieces(chunk, rows, slot_rows):
    found = []
    row = chunk * rows
    while row < (chunk + 1) * rows:
        slot, offset = divmod(row, slot_rows)
        size = min(slot_rows - offset, (chunk + 1) * rows - row)
        found.append((slot, offset, row - chunk * rows, size))
        row += size
    return found


def fetch(fresh, fresh_here, arrived, target, sem):
    moved = pltpu.make_async_copy(arrived, target, sem)
    if fresh is None:
        moved.start()
        moved.wait()
        return

    @pl.when(fresh_here)
    def _():
        for source, at in fresh:
            for copy in spread(source, 0, target, at, sem):
                copy.start()
        moved.wait()

    @pl.when(jnp.logical_not(fresh_here))
    def _():
        moved.start()
        moved.wait()


def block(j, cut):
    return pl.ds(pl.multiple_of(j * cut, cut), cut)


def forward_kernel(
    tick, chunks, sections, place, plan, arrived, inputs, gain, w_in, w_out, *rest
):
    if tick > 0:
        rest = rest[5:]
    send, x_all, aux_all, hidden_all, w_in_t, w_out_t, *rest = rest
    x, aux, hidden, turned, sems = rest
    count, rows, cut = x.shape
    width = count * cut
    inner = w_in.shape[1]
    mine = tick - SKEW * place[0]
    active = jnp.logical_and(mine >= 0, mine < chunks)

    @pl.when(active)
    def _():
        fresh = None
        if tick < chunks:
            fresh = [
                (inputs.at[plan[slot], pl.ds(offset, size), :], at)
                for slot, offset, at, size in pieces(tick, rows, inputs.shape[1])
            ]
        fetch(fresh, place[0] == 0, arrived, x, sems.at[0])
        at = pl.ds(pl.multiple_of(mine * rows, rows), rows)
        store_x = pltpu.make_async_copy(x, x_all.at[:, at, :], sems.at[1])
        store_x.start()

        def project(j, carry):
            total, pre = carry
            value = x[j].astype(F32)
            piece = (value * gain[:, block(j, cut)]).astype(BF16)
            product = jnp.dot(piece, w_in[block(j, cut), :], preferred_element_type=F32)
            return total + value * value, pre + product

        start = jnp.zeros((rows, cut), F32), jnp.zeros((rows, inner), F32)
        total, pre = across(count, project, start)
        inverse = lax.rsqrt(jnp.sum(total, axis=1, keepdims=True) / width + EPSILON)
        pre = pre * inverse
        aux[:, :inner] = pre
        aux[:, inner:] = jnp.broadcast_to(inverse, (rows, AUX))
        store_aux = pltpu.make_async_copy(aux, aux_all.at[at, :], sems.at[2])
        store_aux.start()
        act = (pre / (1.0 + jnp.exp(-pre))).astype(BF16)
        hidden[...] = act
        store_hidden = pltpu.make_async_copy(hidden, hidden_all.at[at, :], sems.at[3])
        store_hidden.start()

        def expand(j, nothing):
            delta = jnp.dot(act, w_out[:, block(j, cut)], preferred_element_type=F32)
            send[j] = (x[j].astype(F32) + delta).astype(BF16)
            return nothing

        across(count, expand, 0)
        store_x.wait()
        store_aux.wait()
        store_hidden.wait()

    idle = SKEW * (sections - 1)

    def turn(j):
        turned[0] = w_in[block(j, cut), :].T
        first = pltpu.make_async_copy(turned.at[0], w_in_t.at[:, block(j, cut)], sems.at[4])
        first.start()
        turned[1] = w_out[:, block(j, cut)].T
        second = pltpu.make_async_copy(turned.at[1], w_out_t.at[block(j, cut), :], sems.at[5])
        second.start()
        first.wait()
        second.wait()

    spare = jnp.where(mine < 0, tick, tick - chunks)
    for again in range(-(-count // idle)):
        j = spare + again * idle

        @pl.when(jnp.logical_and(jnp.logical_not(active), j < count))
        def _():
            turn(j)


def forward_step(
    tick, chunks, rows, sections, count, place, plan, arrived, inputs, gain, w_in, w_out, kept
):
    width, inner = w_in.shape
    cut = width // count
    shapes = (
        jax.ShapeDtypeStruct((count, rows, cut), BF16),
        pltpu.HBM((count, chunks * rows, cut), BF16),
        pltpu.HBM((chunks * rows, inner + AUX), F32),
        pltpu.HBM((chunks * rows, inner), BF16),
        pltpu.HBM((inner, width), BF16),
        pltpu.HBM((width, inner), BF16),
    )
    specs = [smem(), smem(), hbm(), hbm(), vmem(), vmem(), vmem()] + [hbm()] * len(kept)
    return pl.pallas_call(
        functools.partial(forward_kernel, tick, chunks, sections),
        out_shape=shapes,
        in_specs=specs,
        out_specs=(vmem(),) + (hbm(),) * 5,
        scratch_shapes=[
            pltpu.VMEM((count, rows, cut), BF16),
            pltpu.VMEM((rows, inner + AUX), F32),
            pltpu.VMEM((rows, inner), BF16),
            pltpu.VMEM((2, inner, cut), BF16),
            pltpu.SemaphoreType.DMA((6,)),
        ],
        input_output_aliases={7 + k: 1 + k for k in range(len(kept))},
        compiler_params=pltpu.CompilerParams(vmem_limit_bytes=10 << 20),
        cost_estimate=pl.CostEstimate(
            flops=4 * rows * width * inner, bytes_accessed=10 << 20, transcendentals=0
        ),
        name="forward_step",
    )(
        place,
        plan,
        arrived,
        *kept_in(pltpu.HBM, inputs),
        gain,
        *kept_in(pltpu.VMEM, w_in, w_out),
        *kept_in(pltpu.HBM, *kept),
    )


def backward_kernel(
    tick, chunks, sections, held, parts, place, arrived, cotangent, x_all, aux_all, gain, w_in, w_out, *rest
):
    rest = rest[2 * held :]
    send, *rest = rest
    stores, rest = rest[: 2 * parts], rest[2 * parts :]
    up, x, aux, grad, sems = rest
    count, rows, cut = up.shape
    width = count * cut
    inner = w_in.shape[0]
    mine = tick - SKEW * (sections - 1 - place[0])
    active = jnp.logical_and(mine >= 0, mine < chunks)
    share = chunks // PARTS

    def put(value, which, sem):
        lead = PARTS - parts
        for part in range(parts):
            here = mine - (lead + part) * share

            def place_of():
                ref = stores[2 * part + which]
                at = pl.ds(pl.multiple_of(here * rows, rows), rows)
                return ref.at[:, at, :] if which == 0 else ref.at[at, :]

            @pl.when(jnp.logical_and(here >= 0, here < share))
            def _():
                pltpu.make_async_copy(value, place_of(), sem).start()

    @pl.when(active)
    def _():
        at = pl.ds(pl.multiple_of(mine * rows, rows), rows)
        load_x = pltpu.make_async_copy(x_all.at[:, at, :], x, sems.at[1])
        load_x.start()
        load_aux = pltpu.make_async_copy(aux_all.at[at, :], aux, sems.at[2])
        load_aux.start()
        fresh = None
        if tick < chunks:
            fresh = [
                (cotangent.at[slot, pl.ds(offset, size), :], at)
                for slot, offset, at, size in pieces(tick, rows, cotangent.shape[1])
            ]
        fetch(fresh, place[0] == sections - 1, arrived, up, sems.at[0])
        put(up, 0, sems.at[3])

        def project(j, total):
            return total + jnp.dot(up[j], w_out[block(j, cut), :], preferred_element_type=F32)

        grad_hidden = across(count, project, jnp.zeros((rows, inner), F32))
        load_aux.wait()
        pre = aux[:, :inner]
        inverse = aux[:, inner : inner + 1]
        gate = 1.0 / (1.0 + jnp.exp(-pre))
        exact = grad_hidden * gate * (1.0 + pre * (1.0 - gate))
        grad[...] = (exact * inverse).astype(BF16)
        put(grad, 1, sems.at[4])
        grad_pre = exact.astype(BF16)
        mean = jnp.sum(exact * pre, axis=1, keepdims=True) * (inverse / width)
        load_x.wait()

        def expand(j, nothing):
            cols = block(j, cut)
            back = jnp.dot(grad_pre, w_in[:, cols], preferred_element_type=F32)
            inside = back * gain[:, cols] - x[j].astype(F32) * mean
            send[j] = (up[j].astype(F32) + inverse * inside).astype(BF16)
            return nothing

        across(count, expand, 0)
        pltpu.make_async_copy(up, up, sems.at[3]).wait()
        pltpu.make_async_copy(grad, grad, sems.at[4]).wait()


def backward_step(
    tick, chunks, rows, sections, place, arrived, cotangent, x_all, aux_all, gain, w_in, w_out, kept, parts
):
    inner, width = w_in.shape
    count = x_all.shape[0]
    cut = width // count
    share = chunks // PARTS * rows
    shapes = [jax.ShapeDtypeStruct((count, rows, cut), BF16)]
    for _ in range(parts):
        shapes += [pltpu.HBM((count, share, cut), BF16), pltpu.HBM((share, inner), BF16)]
    specs = [smem()] + [hbm()] * 4 + [vmem()] * 3 + [hbm()] * len(kept)
    return pl.pallas_call(
        functools.partial(backward_kernel, tick, chunks, sections, len(kept) // 2, parts),
        out_shape=shapes,
        in_specs=specs,
        out_specs=[vmem()] + [hbm()] * (2 * parts),
        scratch_shapes=[
            pltpu.VMEM((count, rows, cut), BF16),
            pltpu.VMEM((count, rows, cut), BF16),
            pltpu.VMEM((rows, inner + AUX), F32),
            pltpu.VMEM((rows, inner), BF16),
            pltpu.SemaphoreType.DMA((5,)),
        ],
        input_output_aliases={8 + k: 1 + k for k in range(len(kept))},
        compiler_params=pltpu.CompilerParams(vmem_limit_bytes=10 << 20),
        cost_estimate=pl.CostEstimate(
            flops=4 * rows * width * inner, bytes_accessed=10 << 20, transcendentals=0
        ),
        name="backward_step",
    )(
        place,
        arrived,
        *kept_in(pltpu.HBM, cotangent, x_all, aux_all),
        gain,
        *kept_in(pltpu.VMEM, w_in, w_out),
        *kept_in(pltpu.HBM, *kept),
    )


def gathered(array, axis):
    return lax.all_gather(array, axis, axis=0, tiled=True)


def columns(array, axis):
    return lax.all_to_all(array, axis, split_axis=0, concat_axis=0, tiled=True)


def contracted(left, right):
    left = left.reshape(-1, left.shape[-1])
    right = right.reshape(-1, right.shape[-1])
    return lax.dot_general(left, right, (((0,), (0,)), ((), ())), preferred_element_type=F32)


def per_device(inputs, cotangent, plan_order, norm_gain, weight_in, weight_out):
    sections = lax.axis_size("pipe")
    count = lax.axis_size("dp")
    micro_count, row_count, width = inputs.shape
    chunks = CHUNKS
    rows = micro_count * row_count // chunks
    cut = width // count
    last = SKEW * (sections - 1)
    ticks = chunks + last
    onward = [(s, s + 1) for s in range(sections - 1)]
    back = [(s + 1, s) for s in range(sections - 1)]
    place = lax.axis_index("pipe").astype(jnp.int32).reshape(1)
    plan = plan_order.astype(jnp.int32)
    empty = jnp.zeros((count, rows, cut), BF16)

    w_in, w_out = resident(weight_in[0], weight_out[0])
    moving = {}
    kept = ()
    for tick in range(ticks):
        arrived = moving.pop(tick, empty)
        send, *kept = forward_step(
            tick,
            chunks,
            rows,
            sections,
            count,
            place,
            plan,
            arrived,
            inputs,
            norm_gain,
            w_in,
            w_out,
            kept,
        )
        if tick + SKEW < ticks:
            moving[tick + SKEW] = lax.ppermute(send, "pipe", onward)
    x_all, aux_all, hidden_all, w_in_t, w_out_t = kept
    x_cols = columns(x_all, "dp")
    hidden_rows = gathered(hidden_all, "dp")

    w_in, w_out = resident(w_in_t, w_out_t)
    share = chunks // PARTS
    moving = {}
    kept = []
    up_cols = []
    grad_rows = []
    for tick in range(ticks):
        arrived = moving.pop(tick, empty)
        if tick == TIED:
            arrived, x_cols = lax.optimization_barrier((arrived, x_cols))
        parts = PARTS - len(up_cols)
        send, *kept = backward_step(
            tick,
            chunks,
            rows,
            sections,
            place,
            arrived,
            cotangent,
            x_all,
            aux_all,
            norm_gain,
            w_in,
            w_out,
            kept,
            parts,
        )
        if tick + SKEW < ticks:
            moving[tick + SKEW] = lax.ppermute(send, "pipe", back)
        if tick - last + 1 == (len(up_cols) + 1) * share:
            up_cols.append(columns(kept[0], "dp"))
            grad_rows.append(gathered(kept[1], "dp"))
            kept = kept[2:]
    gain = lax.dynamic_slice(norm_gain[0], (lax.axis_index("dp") * cut,), (cut,))
    total_in = 0.0
    total_out = 0.0
    hidden_rows = hidden_rows.reshape(count, PARTS, share * rows, -1)
    x_cols = x_cols.reshape(count, PARTS, share * rows, -1)
    for part in range(PARTS):
        total_in = total_in + contracted(x_cols[:, part], grad_rows[part])
        total_out = total_out + contracted(hidden_rows[:, part], up_cols[part])
    total_in = (total_in * gain[:, None]).astype(BF16)
    return total_in[None], total_out.astype(BF16)[None]


def solution(mesh):
    in_specs = (
        P(None, "dp", None),
        P(None, "dp", None),
        P(),
        P("pipe", None),
        P("pipe", None, None),
        P("pipe", None, None),
    )
    out_specs = (P("pipe", "dp", None), P("pipe", None, "dp"))
    return jax.shard_map(
        per_device, mesh=mesh, in_specs=in_specs, out_specs=out_specs, check_vma=False
    )
```

```python
import functools

import jax
import jax.numpy as jnp
from jax import lax
from jax.experimental import pallas as pl
from jax.experimental.pallas import tpu as pltpu
from jax.sharding import PartitionSpec as P

EPSILON = 1e-05
CHUNKS = 12
SKEW = 2
AUX = 128
TOGETHER = 8

F32 = jnp.float32
BF16 = jnp.bfloat16


def hbm():
    return pl.BlockSpec(memory_space=pltpu.HBM)


def vmem():
    return pl.BlockSpec(memory_space=pltpu.VMEM)


def smem():
    return pl.BlockSpec(memory_space=pltpu.SMEM)


def across(count, body, start):
    def step(j, carry):
        for k in range(TOGETHER):
            carry = body(j * TOGETHER + k, carry)
        return carry

    return lax.fori_loop(0, count // TOGETHER, step, start)


def kept_in(space, *arrays):
    return [pltpu.with_memory_space_constraint(a, space) for a in arrays]


def spread(source, target, at, sem):
    count, _, cut = target.shape
    size = source.shape[0]
    return [
        pltpu.make_async_copy(
            source.at[:, pl.ds(j * cut, cut)], target.at[j, pl.ds(at, size), :], sem
        )
        for j in range(count)
    ]


def pieces(chunk, rows, slot_rows):
    found = []
    row = chunk * rows
    while row < (chunk + 1) * rows:
        slot, offset = divmod(row, slot_rows)
        size = min(slot_rows - offset, (chunk + 1) * rows - row)
        found.append((slot, offset, row - chunk * rows, size))
        row += size
    return found


def fresh(array, chunk, plan, target, sem):
    rows = target.shape[1]
    copies = []
    for slot, offset, at, size in pieces(chunk, rows, array.shape[1]):
        place = plan[slot] if plan is not None else slot
        copies += spread(array.at[place, pl.ds(offset, size), :], target, at, sem)
    return copies


def begin_kernel(plan, first, second, array, first_out, second_out, *rest):
    sems = rest[-1]
    copies = [
        pltpu.make_async_copy(first, first_out, sems.at[0]),
        pltpu.make_async_copy(second, second_out, sems.at[1]),
    ]
    for copy in copies:
        copy.start()
    for chunk, target in enumerate(rest[:-1]):
        for copy in fresh(array, chunk, plan, target, sems.at[2 + chunk]):
            copy.start()
        pltpu.make_async_copy(target, target, sems.at[2 + chunk]).wait()
    for copy in copies:
        copy.wait()


def begin(plan, first, second, array, count, rows):
    chunk = jax.ShapeDtypeStruct((count, rows, array.shape[-1] // count), array.dtype)
    first_out, second_out, *chunks = pl.pallas_call(
        begin_kernel,
        out_shape=(
            pltpu.VMEM(first.shape, first.dtype),
            pltpu.VMEM(second.shape, second.dtype),
        )
        + (chunk,) * SKEW,
        in_specs=[smem()] + [hbm()] * 3,
        out_specs=(vmem(),) * (2 + SKEW),
        scratch_shapes=[pltpu.SemaphoreType.DMA((2 + SKEW,))],
        compiler_params=pltpu.CompilerParams(vmem_limit_bytes=3 << 20),
        name="begin",
    )(plan, *kept_in(pltpu.HBM, first, second, array))
    return first_out, second_out, chunks


def block(j, cut):
    return pl.ds(pl.multiple_of(j * cut, cut), cut)


def forward_kernel(
    tick, chunks, sections, place, plan, arrived, inputs, gain, w_in, w_out, *rest
):
    if tick > 0:
        rest = rest[5:]
    send, x_all, aux_all, hidden_all, w_in_t, w_out_t, *rest = rest
    aux, hidden, turned, sems = rest
    x = arrived
    count, rows, cut = x.shape
    width = count * cut
    inner = w_in.shape[1]
    mine = tick - SKEW * place[0]
    active = jnp.logical_and(mine >= 0, mine < chunks)

    at_end = place[0] == sections - 1
    feeding = tick + SKEW < chunks
    if feeding:

        @pl.when(at_end)
        def _():
            for copy in fresh(inputs, tick + SKEW, plan, send, sems.at[0]):
                copy.start()

    @pl.when(active)
    def _():
        at = pl.ds(pl.multiple_of(mine * rows, rows), rows)
        store_x = pltpu.make_async_copy(x, x_all.at[:, at, :], sems.at[1])
        store_x.start()

        def project(j, carry):
            total, pre = carry
            value = x[j].astype(F32)
            piece = (value * gain[:, block(j, cut)]).astype(BF16)
            product = jnp.dot(piece, w_in[block(j, cut), :], preferred_element_type=F32)
            return total + value * value, pre + product

        start = jnp.zeros((rows, cut), F32), jnp.zeros((rows, inner), F32)
        total, pre = across(count, project, start)
        inverse = lax.rsqrt(jnp.sum(total, axis=1, keepdims=True) / width + EPSILON)
        pre = pre * inverse
        aux[:, :inner] = pre
        aux[:, inner:] = jnp.broadcast_to(inverse, (rows, AUX))
        store_aux = pltpu.make_async_copy(aux, aux_all.at[at, :], sems.at[2])
        store_aux.start()
        act = (pre / (1.0 + jnp.exp(-pre))).astype(BF16)
        hidden[...] = act
        store_hidden = pltpu.make_async_copy(hidden, hidden_all.at[at, :], sems.at[3])
        store_hidden.start()

        def expand(j, nothing):
            delta = jnp.dot(act, w_out[:, block(j, cut)], preferred_element_type=F32)
            send[j] = (x[j].astype(F32) + delta).astype(BF16)
            return nothing

        @pl.when(jnp.logical_not(at_end))
        def _():
            across(count, expand, 0)

        store_x.wait()
        store_aux.wait()
        store_hidden.wait()

    idle = SKEW * (sections - 1)

    def turn(j):
        turned[0] = w_in[block(j, cut), :].T
        first = pltpu.make_async_copy(turned.at[0], w_in_t.at[:, block(j, cut)], sems.at[4])
        first.start()
        turned[1] = w_out[:, block(j, cut)].T
        second = pltpu.make_async_copy(turned.at[1], w_out_t.at[block(j, cut), :], sems.at[5])
        second.start()
        first.wait()
        second.wait()

    spare = jnp.where(mine < 0, tick, tick - chunks)
    for again in range(-(-count // idle)):
        j = spare + again * idle

        @pl.when(jnp.logical_and(jnp.logical_not(active), j < count))
        def _():
            turn(j)

    if feeding:

        @pl.when(at_end)
        def _():
            pltpu.make_async_copy(send, send, sems.at[0]).wait()


def forward_step(
    tick, chunks, rows, sections, count, place, plan, arrived, inputs, gain, w_in, w_out, kept
):
    width, inner = w_in.shape
    cut = width // count
    shapes = (
        jax.ShapeDtypeStruct((count, rows, cut), BF16),
        pltpu.HBM((count, chunks * rows, cut), BF16),
        pltpu.HBM((chunks * rows, inner + AUX), F32),
        pltpu.HBM((chunks * rows, inner), BF16),
        pltpu.HBM((inner, width), BF16),
        pltpu.HBM((width, inner), BF16),
    )
    specs = [smem(), smem(), vmem(), hbm(), vmem(), vmem(), vmem()] + [hbm()] * len(kept)
    return pl.pallas_call(
        functools.partial(forward_kernel, tick, chunks, sections),
        out_shape=shapes,
        in_specs=specs,
        out_specs=(vmem(),) + (hbm(),) * 5,
        scratch_shapes=[
            pltpu.VMEM((rows, inner + AUX), F32),
            pltpu.VMEM((rows, inner), BF16),
            pltpu.VMEM((2, inner, cut), BF16),
            pltpu.SemaphoreType.DMA((6,)),
        ],
        input_output_aliases={7 + k: 1 + k for k in range(len(kept))},
        compiler_params=pltpu.CompilerParams(vmem_limit_bytes=10 << 20),
        cost_estimate=pl.CostEstimate(
            flops=4 * rows * width * inner, bytes_accessed=10 << 20, transcendentals=0
        ),
        name="forward_step",
    )(
        place,
        plan,
        arrived,
        *kept_in(pltpu.HBM, inputs),
        gain,
        *kept_in(pltpu.VMEM, w_in, w_out),
        *kept_in(pltpu.HBM, *kept),
    )


def backward_kernel(
    tick, chunks, sections, place, arrived, cotangent, x_all, aux_all, gain, w_in, w_out, *rest
):
    if tick > 0:
        rest = rest[2:]
    send, up_all, grad_all, x, aux, grad, sems = rest
    up = arrived
    count, rows, cut = up.shape
    width = count * cut
    inner = w_in.shape[0]
    mine = tick - SKEW * (sections - 1 - place[0])
    active = jnp.logical_and(mine >= 0, mine < chunks)
    at_end = place[0] == 0
    feeding = tick + SKEW < chunks
    if feeding:

        @pl.when(at_end)
        def _():
            for copy in fresh(cotangent, tick + SKEW, None, send, sems.at[0]):
                copy.start()

    @pl.when(active)
    def _():
        at = pl.ds(pl.multiple_of(mine * rows, rows), rows)
        load_x = pltpu.make_async_copy(x_all.at[:, at, :], x, sems.at[1])
        load_x.start()
        load_aux = pltpu.make_async_copy(aux_all.at[at, :], aux, sems.at[2])
        load_aux.start()
        store_up = pltpu.make_async_copy(up, up_all.at[:, at, :], sems.at[3])
        store_up.start()

        def project(j, total):
            return total + jnp.dot(up[j], w_out[block(j, cut), :], preferred_element_type=F32)

        grad_hidden = across(count, project, jnp.zeros((rows, inner), F32))
        load_aux.wait()
        pre = aux[:, :inner]
        inverse = aux[:, inner : inner + 1]
        gate = 1.0 / (1.0 + jnp.exp(-pre))
        exact = grad_hidden * gate * (1.0 + pre * (1.0 - gate))
        grad[...] = (exact * inverse).astype(BF16)
        store_grad = pltpu.make_async_copy(grad, grad_all.at[at, :], sems.at[4])
        store_grad.start()
        grad_pre = exact.astype(BF16)
        mean = jnp.sum(exact * pre, axis=1, keepdims=True) * (inverse / width)
        load_x.wait()

        def expand(j, nothing):
            cols = block(j, cut)
            back = jnp.dot(grad_pre, w_in[:, cols], preferred_element_type=F32)
            inside = back * gain[:, cols] - x[j].astype(F32) * mean
            send[j] = (up[j].astype(F32) + inverse * inside).astype(BF16)
            return nothing

        @pl.when(jnp.logical_not(at_end))
        def _():
            across(count, expand, 0)

        store_up.wait()
        store_grad.wait()

    if feeding:

        @pl.when(at_end)
        def _():
            pltpu.make_async_copy(send, send, sems.at[0]).wait()


def backward_step(
    tick, chunks, rows, sections, place, arrived, cotangent, x_all, aux_all, gain, w_in, w_out, kept
):
    inner, width = w_in.shape
    count = x_all.shape[0]
    cut = width // count
    shapes = (
        jax.ShapeDtypeStruct((count, rows, cut), BF16),
        pltpu.HBM((count, chunks * rows, cut), BF16),
        pltpu.HBM((chunks * rows, inner), BF16),
    )
    specs = [smem(), vmem()] + [hbm()] * 3 + [vmem()] * 3 + [hbm()] * len(kept)
    return pl.pallas_call(
        functools.partial(backward_kernel, tick, chunks, sections),
        out_shape=shapes,
        in_specs=specs,
        out_specs=(vmem(), hbm(), hbm()),
        scratch_shapes=[
            pltpu.VMEM((count, rows, cut), BF16),
            pltpu.VMEM((rows, inner + AUX), F32),
            pltpu.VMEM((rows, inner), BF16),
            pltpu.SemaphoreType.DMA((5,)),
        ],
        input_output_aliases={8 + k: 1 + k for k in range(len(kept))},
        compiler_params=pltpu.CompilerParams(vmem_limit_bytes=10 << 20),
        cost_estimate=pl.CostEstimate(
            flops=4 * rows * width * inner, bytes_accessed=10 << 20, transcendentals=0
        ),
        name="backward_step",
    )(
        place,
        arrived,
        *kept_in(pltpu.HBM, cotangent, x_all, aux_all),
        gain,
        *kept_in(pltpu.VMEM, w_in, w_out),
        *kept_in(pltpu.HBM, *kept),
    )


def gathered(array, axis):
    return lax.all_gather(array, axis, axis=0, tiled=True)


def columns(array, axis):
    return lax.all_to_all(array, axis, split_axis=0, concat_axis=0, tiled=True)


def contracted(left, right):
    left = left.reshape(-1, left.shape[-1])
    right = right.reshape(-1, right.shape[-1])
    return lax.dot_general(left, right, (((0,), (0,)), ((), ())), preferred_element_type=F32)


def per_device(inputs, cotangent, plan_order, norm_gain, weight_in, weight_out):
    sections = lax.axis_size("pipe")
    count = lax.axis_size("dp")
    micro_count, row_count, width = inputs.shape
    chunks = CHUNKS
    rows = micro_count * row_count // chunks
    cut = width // count
    last = SKEW * (sections - 1)
    ticks = chunks + last
    onward = [(s, (s + 1) % sections) for s in range(sections)]
    back = [(after, s) for s, after in onward]
    place = lax.axis_index("pipe").astype(jnp.int32).reshape(1)
    plan = plan_order.astype(jnp.int32)

    w_in, w_out, early = begin(plan, weight_in[0], weight_out[0], inputs, count, rows)
    moving = dict(enumerate(early))
    kept = ()
    for tick in range(ticks):
        arrived = moving.pop(tick)
        send, *kept = forward_step(
            tick,
            chunks,
            rows,
            sections,
            count,
            place,
            plan,
            arrived,
            inputs,
            norm_gain,
            w_in,
            w_out,
            kept,
        )
        if tick + SKEW < ticks:
            moving[tick + SKEW] = lax.ppermute(send, "pipe", onward)
    x_all, aux_all, hidden_all, w_in_t, w_out_t = kept
    hidden_rows = gathered(hidden_all, "dp")

    order = jnp.arange(micro_count, dtype=jnp.int32)
    w_in, w_out, early = begin(order, w_in_t, w_out_t, cotangent, count, rows)
    moving = dict(enumerate(early))
    kept = ()
    for tick in range(ticks):
        arrived = moving.pop(tick)
        send, *kept = backward_step(
            tick,
            chunks,
            rows,
            sections,
            place,
            arrived,
            cotangent,
            x_all,
            aux_all,
            norm_gain,
            w_in,
            w_out,
            kept,
        )
        if tick + SKEW < ticks:
            moving[tick + SKEW] = lax.ppermute(send, "pipe", back)
    up_all, grad_all = kept
    x_all, up_all = lax.optimization_barrier((x_all, up_all))
    x_cols, up_cols = lax.optimization_barrier((columns(x_all, "dp"), columns(up_all, "dp")))
    grad_rows = gathered(grad_all, "dp")
    gain = lax.dynamic_slice(norm_gain[0], (lax.axis_index("dp") * cut,), (cut,))
    total_in = contracted(x_cols, grad_rows) * gain[:, None]
    total_out = contracted(hidden_rows, up_cols)
    return total_in.astype(BF16)[None], total_out.astype(BF16)[None]


def solution(mesh):
    in_specs = (
        P(None, "dp", None),
        P(None, "dp", None),
        P(),
        P("pipe", None),
        P("pipe", None, None),
        P("pipe", None, None),
    )
    out_specs = (P("pipe", "dp", None), P("pipe", None, "dp"))
    return jax.shard_map(
        per_device, mesh=mesh, in_specs=in_specs, out_specs=out_specs, check_vma=False
    )
```

```python
import functools

import jax
import jax.numpy as jnp
from jax import lax
from jax.experimental import pallas as pl
from jax.experimental.pallas import tpu as pltpu
from jax.sharding import PartitionSpec as P

EPSILON = 1e-05
CHUNKS = 12
SKEW = 2
AUX = 128
TOGETHER = 8

F32 = jnp.float32
BF16 = jnp.bfloat16


def hbm():
    return pl.BlockSpec(memory_space=pltpu.HBM)


def vmem():
    return pl.BlockSpec(memory_space=pltpu.VMEM)


def smem():
    return pl.BlockSpec(memory_space=pltpu.SMEM)


def across(count, body, start):
    def step(j, carry):
        for k in range(TOGETHER):
            carry = body(j * TOGETHER + k, carry)
        return carry

    return lax.fori_loop(0, count // TOGETHER, step, start)


def kept_in(space, *arrays):
    return [pltpu.with_memory_space_constraint(a, space) for a in arrays]


def spread(source, target, at, sem):
    count, _, cut = target.shape
    size = source.shape[0]
    return [
        pltpu.make_async_copy(
            source.at[:, pl.ds(j * cut, cut)], target.at[j, pl.ds(at, size), :], sem
        )
        for j in range(count)
    ]


def pieces(chunk, rows, slot_rows):
    found = []
    row = chunk * rows
    while row < (chunk + 1) * rows:
        slot, offset = divmod(row, slot_rows)
        size = min(slot_rows - offset, (chunk + 1) * rows - row)
        found.append((slot, offset, row - chunk * rows, size))
        row += size
    return found


def fresh(array, chunk, plan, target, sem):
    rows = target.shape[1]
    copies = []
    for slot, offset, at, size in pieces(chunk, rows, array.shape[1]):
        place = plan[slot] if plan is not None else slot
        copies += spread(array.at[place, pl.ds(offset, size), :], target, at, sem)
    return copies


def begin_kernel(plan, first, second, array, first_out, second_out, *rest):
    sems = rest[-1]
    copies = [
        pltpu.make_async_copy(first, first_out, sems.at[0]),
        pltpu.make_async_copy(second, second_out, sems.at[1]),
    ]
    for copy in copies:
        copy.start()
    for chunk, target in enumerate(rest[:-1]):
        for copy in fresh(array, chunk, plan, target, sems.at[2 + chunk]):
            copy.start()
        pltpu.make_async_copy(target, target, sems.at[2 + chunk]).wait()
    for copy in copies:
        copy.wait()


def begin(plan, first, second, array, count, rows):
    chunk = jax.ShapeDtypeStruct((count, rows, array.shape[-1] // count), array.dtype)
    first_out, second_out, *chunks = pl.pallas_call(
        begin_kernel,
        out_shape=(
            pltpu.VMEM(first.shape, first.dtype),
            pltpu.VMEM(second.shape, second.dtype),
        )
        + (chunk,) * SKEW,
        in_specs=[smem()] + [hbm()] * 3,
        out_specs=(vmem(),) * (2 + SKEW),
        scratch_shapes=[pltpu.SemaphoreType.DMA((2 + SKEW,))],
        compiler_params=pltpu.CompilerParams(vmem_limit_bytes=3 << 20),
        name="begin",
    )(plan, *kept_in(pltpu.HBM, first, second, array))
    return first_out, second_out, chunks


def block(j, cut):
    return pl.ds(pl.multiple_of(j * cut, cut), cut)


def forward_kernel(
    tick, chunks, sections, place, plan, arrived, inputs, gain, w_in, w_out, *rest
):
    if tick > 0:
        rest = rest[5:]
    send, x_all, aux_all, hidden_all, w_in_t, w_out_t, *rest = rest
    aux, hidden, turned, sems = rest
    x = arrived
    count, rows, cut = x.shape
    width = count * cut
    inner = w_in.shape[1]
    mine = tick - SKEW * place[0]
    active = jnp.logical_and(mine >= 0, mine < chunks)

    at_end = place[0] == sections - 1
    feeding = tick + SKEW < chunks
    if feeding:

        @pl.when(at_end)
        def _():
            for copy in fresh(inputs, tick + SKEW, plan, send, sems.at[0]):
                copy.start()

    @pl.when(active)
    def _():
        at = pl.ds(pl.multiple_of(mine * rows, rows), rows)
        store_x = pltpu.make_async_copy(x, x_all.at[:, at, :], sems.at[1])
        store_x.start()

        def project(j, carry):
            total, pre = carry
            value = x[j].astype(F32)
            piece = (value * gain[:, block(j, cut)]).astype(BF16)
            product = jnp.dot(piece, w_in[block(j, cut), :], preferred_element_type=F32)
            return total + value * value, pre + product

        start = jnp.zeros((rows, cut), F32), jnp.zeros((rows, inner), F32)
        total, pre = across(count, project, start)
        inverse = lax.rsqrt(jnp.sum(total, axis=1, keepdims=True) / width + EPSILON)
        pre = pre * inverse
        aux[:, :inner] = pre
        aux[:, inner:] = jnp.broadcast_to(inverse, (rows, AUX))
        store_aux = pltpu.make_async_copy(aux, aux_all.at[at, :], sems.at[2])
        store_aux.start()
        act = (pre / (1.0 + jnp.exp(-pre))).astype(BF16)
        hidden[...] = act
        store_hidden = pltpu.make_async_copy(hidden, hidden_all.at[at, :], sems.at[3])
        store_hidden.start()

        def expand(j, nothing):
            delta = jnp.dot(act, w_out[:, block(j, cut)], preferred_element_type=F32)
            send[j] = (x[j].astype(F32) + delta).astype(BF16)
            return nothing

        @pl.when(jnp.logical_not(at_end))
        def _():
            across(count, expand, 0)

        store_x.wait()
        store_aux.wait()
        store_hidden.wait()

    idle = SKEW * (sections - 1)

    def turn(j):
        turned[0] = w_in[block(j, cut), :].T
        first = pltpu.make_async_copy(turned.at[0], w_in_t.at[:, block(j, cut)], sems.at[4])
        first.start()
        turned[1] = w_out[:, block(j, cut)].T
        second = pltpu.make_async_copy(turned.at[1], w_out_t.at[block(j, cut), :], sems.at[5])
        second.start()
        first.wait()
        second.wait()

    spare = jnp.where(mine < 0, tick, tick - chunks)
    for again in range(-(-count // idle)):
        j = spare + again * idle

        @pl.when(jnp.logical_and(jnp.logical_not(active), j < count))
        def _():
            turn(j)

    if feeding:

        @pl.when(at_end)
        def _():
            pltpu.make_async_copy(send, send, sems.at[0]).wait()


def forward_step(
    tick, chunks, rows, sections, count, place, plan, arrived, inputs, gain, w_in, w_out, kept
):
    width, inner = w_in.shape
    cut = width // count
    shapes = (
        jax.ShapeDtypeStruct((count, rows, cut), BF16),
        pltpu.HBM((count, 2 * chunks * rows, cut), BF16),
        pltpu.HBM((chunks * rows, inner + AUX), F32),
        pltpu.HBM((chunks * rows, inner), BF16),
        pltpu.HBM((inner, width), BF16),
        pltpu.HBM((width, inner), BF16),
    )
    specs = [smem(), smem(), vmem(), hbm(), vmem(), vmem(), vmem()] + [hbm()] * len(kept)
    return pl.pallas_call(
        functools.partial(forward_kernel, tick, chunks, sections),
        out_shape=shapes,
        in_specs=specs,
        out_specs=(vmem(),) + (hbm(),) * 5,
        scratch_shapes=[
            pltpu.VMEM((rows, inner + AUX), F32),
            pltpu.VMEM((rows, inner), BF16),
            pltpu.VMEM((2, inner, cut), BF16),
            pltpu.SemaphoreType.DMA((6,)),
        ],
        input_output_aliases={7 + k: 1 + k for k in range(len(kept))},
        compiler_params=pltpu.CompilerParams(vmem_limit_bytes=10 << 20),
        cost_estimate=pl.CostEstimate(
            flops=4 * rows * width * inner, bytes_accessed=10 << 20, transcendentals=0
        ),
        name="forward_step",
    )(
        place,
        plan,
        arrived,
        *kept_in(pltpu.HBM, inputs),
        gain,
        *kept_in(pltpu.VMEM, w_in, w_out),
        *kept_in(pltpu.HBM, *kept),
    )


def backward_kernel(
    tick, chunks, sections, place, arrived, cotangent, aux_all, gain, w_in, w_out, *rest
):
    send, rows_all, grad_all, x, aux, grad, sems = rest[1 if tick == 0 else 2 :]
    up = arrived
    count, rows, cut = up.shape
    width = count * cut
    inner = w_in.shape[0]
    mine = tick - SKEW * (sections - 1 - place[0])
    active = jnp.logical_and(mine >= 0, mine < chunks)
    at_end = place[0] == 0
    feeding = tick + SKEW < chunks
    if feeding:

        @pl.when(at_end)
        def _():
            for copy in fresh(cotangent, tick + SKEW, None, send, sems.at[0]):
                copy.start()

    @pl.when(active)
    def _():
        at = pl.ds(pl.multiple_of(mine * rows, rows), rows)
        load_x = pltpu.make_async_copy(rows_all.at[:, at, :], x, sems.at[1])
        load_x.start()
        load_aux = pltpu.make_async_copy(aux_all.at[at, :], aux, sems.at[2])
        load_aux.start()
        behind = pl.ds(pl.multiple_of((mine + chunks) * rows, rows), rows)
        store_up = pltpu.make_async_copy(up, rows_all.at[:, behind, :], sems.at[3])
        store_up.start()

        def project(j, total):
            return total + jnp.dot(up[j], w_out[block(j, cut), :], preferred_element_type=F32)

        grad_hidden = across(count, project, jnp.zeros((rows, inner), F32))
        load_aux.wait()
        pre = aux[:, :inner]
        inverse = aux[:, inner : inner + 1]
        gate = 1.0 / (1.0 + jnp.exp(-pre))
        exact = grad_hidden * gate * (1.0 + pre * (1.0 - gate))
        grad[...] = (exact * inverse).astype(BF16)
        store_grad = pltpu.make_async_copy(grad, grad_all.at[at, :], sems.at[4])
        store_grad.start()
        grad_pre = exact.astype(BF16)
        mean = jnp.sum(exact * pre, axis=1, keepdims=True) * (inverse / width)
        load_x.wait()

        def expand(j, nothing):
            cols = block(j, cut)
            back = jnp.dot(grad_pre, w_in[:, cols], preferred_element_type=F32)
            inside = back * gain[:, cols] - x[j].astype(F32) * mean
            send[j] = (up[j].astype(F32) + inverse * inside).astype(BF16)
            return nothing

        @pl.when(jnp.logical_not(at_end))
        def _():
            across(count, expand, 0)

        store_up.wait()
        store_grad.wait()

    if feeding:

        @pl.when(at_end)
        def _():
            pltpu.make_async_copy(send, send, sems.at[0]).wait()


def backward_step(
    tick, chunks, rows, sections, place, arrived, cotangent, aux_all, gain, w_in, w_out, kept
):
    inner, width = w_in.shape
    count = kept[0].shape[0]
    cut = width // count
    shapes = (
        jax.ShapeDtypeStruct((count, rows, cut), BF16),
        pltpu.HBM((count, 2 * chunks * rows, cut), BF16),
        pltpu.HBM((chunks * rows, inner), BF16),
    )
    specs = [smem(), vmem()] + [hbm()] * 2 + [vmem()] * 3 + [hbm()] * len(kept)
    return pl.pallas_call(
        functools.partial(backward_kernel, tick, chunks, sections),
        out_shape=shapes,
        in_specs=specs,
        out_specs=(vmem(), hbm(), hbm()),
        scratch_shapes=[
            pltpu.VMEM((count, rows, cut), BF16),
            pltpu.VMEM((rows, inner + AUX), F32),
            pltpu.VMEM((rows, inner), BF16),
            pltpu.SemaphoreType.DMA((5,)),
        ],
        input_output_aliases={7 + k: 1 + k for k in range(len(kept))},
        compiler_params=pltpu.CompilerParams(vmem_limit_bytes=10 << 20),
        cost_estimate=pl.CostEstimate(
            flops=4 * rows * width * inner, bytes_accessed=10 << 20, transcendentals=0
        ),
        name="backward_step",
    )(
        place,
        arrived,
        *kept_in(pltpu.HBM, cotangent, aux_all),
        gain,
        *kept_in(pltpu.VMEM, w_in, w_out),
        *kept_in(pltpu.HBM, *kept),
    )


def gathered(array, axis):
    return lax.all_gather(array, axis, axis=0, tiled=True)


def columns(array, axis):
    return lax.all_to_all(array, axis, split_axis=0, concat_axis=0, tiled=True)


def gradient_kernel(x, up, grad, hidden, gain, grad_in, grad_out, total_in, total_out):
    step = pl.program_id(0)

    @pl.when(step == 0)
    def _():
        total_in[...] = jnp.zeros_like(total_in)
        total_out[...] = jnp.zeros_like(total_out)

    rows = (((0,), (0,)), ((), ()))
    total_in[...] += lax.dot_general(x[0], grad[...], rows, preferred_element_type=F32)
    total_out[...] += lax.dot_general(hidden[...], up[0], rows, preferred_element_type=F32)

    @pl.when(step == pl.num_programs(0) - 1)
    def _():
        grad_in[...] = (total_in[...] * gain[...]).astype(BF16)
        grad_out[...] = total_out[...].astype(BF16)


def gradients(taken, grad_rows, hidden_rows, gain):
    count, both, cut = taken.shape
    tokens = both // 2
    inner = grad_rows.shape[1]
    return pl.pallas_call(
        gradient_kernel,
        grid=(count,),
        out_shape=(
            jax.ShapeDtypeStruct((cut, inner), BF16),
            jax.ShapeDtypeStruct((inner, cut), BF16),
        ),
        in_specs=[
            pl.BlockSpec((1, tokens, cut), lambda q: (q, 0, 0)),
            pl.BlockSpec((1, tokens, cut), lambda q: (q, 1, 0)),
            pl.BlockSpec((tokens, inner), lambda q: (q, 0)),
            pl.BlockSpec((tokens, inner), lambda q: (q, 0)),
            pl.BlockSpec((cut, 1), lambda q: (0, 0)),
        ],
        out_specs=(
            pl.BlockSpec((cut, inner), lambda q: (0, 0)),
            pl.BlockSpec((inner, cut), lambda q: (0, 0)),
        ),
        scratch_shapes=[pltpu.VMEM((cut, inner), F32), pltpu.VMEM((inner, cut), F32)],
        compiler_params=pltpu.CompilerParams(vmem_limit_bytes=24 << 20),
        cost_estimate=pl.CostEstimate(
            flops=4 * count * tokens * cut * inner, bytes_accessed=14 << 20, transcendentals=0
        ),
        name="gradients",
    )(*kept_in(pltpu.HBM, taken, taken, grad_rows, hidden_rows), gain)


def per_device(inputs, cotangent, plan_order, norm_gain, weight_in, weight_out):
    sections = lax.axis_size("pipe")
    count = lax.axis_size("dp")
    micro_count, row_count, width = inputs.shape
    chunks = CHUNKS
    rows = micro_count * row_count // chunks
    cut = width // count
    last = SKEW * (sections - 1)
    ticks = chunks + last
    onward = [(s, (s + 1) % sections) for s in range(sections)]
    back = [(after, s) for s, after in onward]
    place = lax.axis_index("pipe").astype(jnp.int32).reshape(1)
    plan = plan_order.astype(jnp.int32)

    w_in, w_out, early = begin(plan, weight_in[0], weight_out[0], inputs, count, rows)
    moving = dict(enumerate(early))
    kept = ()
    for tick in range(ticks):
        arrived = moving.pop(tick)
        send, *kept = forward_step(
            tick,
            chunks,
            rows,
            sections,
            count,
            place,
            plan,
            arrived,
            inputs,
            norm_gain,
            w_in,
            w_out,
            kept,
        )
        if tick + SKEW < ticks:
            moving[tick + SKEW] = lax.ppermute(send, "pipe", onward)
    rows_all, aux_all, hidden_all, w_in_t, w_out_t = kept
    hidden_rows = gathered(hidden_all, "dp")

    order = jnp.arange(micro_count, dtype=jnp.int32)
    w_in, w_out, early = begin(order, w_in_t, w_out_t, cotangent, count, rows)
    moving = dict(enumerate(early))
    kept = (rows_all,)
    for tick in range(ticks):
        arrived = moving.pop(tick)
        send, *kept = backward_step(
            tick,
            chunks,
            rows,
            sections,
            place,
            arrived,
            cotangent,
            aux_all,
            norm_gain,
            w_in,
            w_out,
            kept,
        )
        if tick + SKEW < ticks:
            moving[tick + SKEW] = lax.ppermute(send, "pipe", back)
    rows_all, grad_all = kept
    taken = columns(rows_all, "dp")
    grad_rows = gathered(grad_all, "dp")
    gain = lax.dynamic_slice(norm_gain[0], (lax.axis_index("dp") * cut,), (cut,))
    grad_in, grad_out = gradients(taken, grad_rows, hidden_rows, gain[:, None])
    return grad_in[None], grad_out[None]


def solution(mesh):
    in_specs = (
        P(None, "dp", None),
        P(None, "dp", None),
        P(),
        P("pipe", None),
        P("pipe", None, None),
        P("pipe", None, None),
    )
    out_specs = (P("pipe", "dp", None), P("pipe", None, "dp"))
    return jax.shard_map(
        per_device, mesh=mesh, in_specs=in_specs, out_specs=out_specs, check_vma=False
    )
```

```python
import functools

import jax
import jax.numpy as jnp
from jax import lax
from jax.experimental import pallas as pl
from jax.experimental.pallas import tpu as pltpu
from jax.sharding import PartitionSpec as P

EPSILON = 1e-05
CHUNKS = 12
TAKEN = 2
GAP = 2
LATER = 4
CORES = 2
SKEW = 2
AUX = 128
TOGETHER = 8

F32 = jnp.float32
BF16 = jnp.bfloat16


def hbm():
    return pl.BlockSpec(memory_space=pltpu.HBM)


def vmem():
    return pl.BlockSpec(memory_space=pltpu.VMEM)


def smem():
    return pl.BlockSpec(memory_space=pltpu.SMEM)


def across(count, body, start):
    def step(j, carry):
        for k in range(TOGETHER):
            carry = body(j * TOGETHER + k, carry)
        return carry

    return lax.fori_loop(0, count // TOGETHER, step, start)


def kept_in(space, *arrays):
    return [pltpu.with_memory_space_constraint(a, space) for a in arrays]


def spread(source, target, at, sem):
    count, _, cut = target.shape
    size = source.shape[0]
    return [
        pltpu.make_async_copy(
            source.at[:, pl.ds(j * cut, cut)], target.at[j, pl.ds(at, size), :], sem
        )
        for j in range(count)
    ]


def pieces(chunk, rows, slot_rows):
    found = []
    row = chunk * rows
    while row < (chunk + 1) * rows:
        slot, offset = divmod(row, slot_rows)
        size = min(slot_rows - offset, (chunk + 1) * rows - row)
        found.append((slot, offset, row - chunk * rows, size))
        row += size
    return found


def fresh(array, chunk, plan, target, sem):
    rows = target.shape[1]
    copies = []
    for slot, offset, at, size in pieces(chunk, rows, array.shape[1]):
        place = plan[slot] if plan is not None else slot
        copies += spread(array.at[place, pl.ds(offset, size), :], target, at, sem)
    return copies


def begin_kernel(plan, first, second, array, first_out, second_out, *rest):
    sems = rest[-1]
    copies = [
        pltpu.make_async_copy(first, first_out, sems.at[0]),
        pltpu.make_async_copy(second, second_out, sems.at[1]),
    ]
    for copy in copies:
        copy.start()
    for chunk, target in enumerate(rest[:-1]):
        for copy in fresh(array, chunk, plan, target, sems.at[2 + chunk]):
            copy.start()
        pltpu.make_async_copy(target, target, sems.at[2 + chunk]).wait()
    for copy in copies:
        copy.wait()


def begin(plan, first, second, array, count, rows):
    chunk = jax.ShapeDtypeStruct((count, rows, array.shape[-1] // count), array.dtype)
    first_out, second_out, *chunks = pl.pallas_call(
        begin_kernel,
        out_shape=(
            pltpu.VMEM(first.shape, first.dtype),
            pltpu.VMEM(second.shape, second.dtype),
        )
        + (chunk,) * SKEW,
        in_specs=[smem()] + [hbm()] * 3,
        out_specs=(vmem(),) * (2 + SKEW),
        scratch_shapes=[pltpu.SemaphoreType.DMA((2 + SKEW,))],
        compiler_params=pltpu.CompilerParams(vmem_limit_bytes=3 << 20),
        name="begin",
    )(plan, *kept_in(pltpu.HBM, first, second, array))
    return first_out, second_out, chunks


def block(j, cut):
    return pl.ds(pl.multiple_of(j * cut, cut), cut)


def forward_kernel(
    tick, chunks, sections, place, plan, arrived, inputs, gain, w_in, w_out, *rest
):
    if tick > 0:
        rest = rest[5:]
    send, x_all, aux_all, hidden_all, w_in_t, w_out_t, *rest = rest
    aux, hidden, turned, sems = rest
    x = arrived
    count, rows, cut = x.shape
    width = count * cut
    inner = w_in.shape[1]
    mine = tick - SKEW * place[0]
    active = jnp.logical_and(mine >= 0, mine < chunks)

    at_end = place[0] == sections - 1
    feeding = tick + SKEW < chunks
    if feeding:

        @pl.when(at_end)
        def _():
            for copy in fresh(inputs, tick + SKEW, plan, send, sems.at[0]):
                copy.start()

    @pl.when(active)
    def _():
        at = pl.ds(pl.multiple_of(mine * rows, rows), rows)
        store_x = pltpu.make_async_copy(x, x_all.at[:, at, :], sems.at[1])
        store_x.start()

        def project(j, carry):
            total, pre = carry
            value = x[j].astype(F32)
            piece = (value * gain[:, block(j, cut)]).astype(BF16)
            product = jnp.dot(piece, w_in[block(j, cut), :], preferred_element_type=F32)
            return total + value * value, pre + product

        start = jnp.zeros((rows, cut), F32), jnp.zeros((rows, inner), F32)
        total, pre = across(count, project, start)
        inverse = lax.rsqrt(jnp.sum(total, axis=1, keepdims=True) / width + EPSILON)
        pre = pre * inverse
        aux[:, :inner] = pre
        aux[:, inner:] = jnp.broadcast_to(inverse, (rows, AUX))
        store_aux = pltpu.make_async_copy(aux, aux_all.at[at, :], sems.at[2])
        store_aux.start()
        act = (pre / (1.0 + jnp.exp(-pre))).astype(BF16)
        hidden[...] = act
        store_hidden = pltpu.make_async_copy(hidden, hidden_all.at[at, :], sems.at[3])
        store_hidden.start()

        def expand(j, nothing):
            delta = jnp.dot(act, w_out[:, block(j, cut)], preferred_element_type=F32)
            send[j] = (x[j].astype(F32) + delta).astype(BF16)
            return nothing

        @pl.when(jnp.logical_not(at_end))
        def _():
            across(count, expand, 0)

        store_x.wait()
        store_aux.wait()
        store_hidden.wait()

    idle = SKEW * (sections - 1)

    def turn(j):
        turned[0] = w_in[block(j, cut), :].T
        first = pltpu.make_async_copy(turned.at[0], w_in_t.at[:, block(j, cut)], sems.at[4])
        first.start()
        turned[1] = w_out[:, block(j, cut)].T
        second = pltpu.make_async_copy(turned.at[1], w_out_t.at[block(j, cut), :], sems.at[5])
        second.start()
        first.wait()
        second.wait()

    spare = jnp.where(mine < 0, tick, tick - chunks)
    for again in range(-(-count // idle)):
        j = spare + again * idle

        @pl.when(jnp.logical_and(jnp.logical_not(active), j < count))
        def _():
            turn(j)

    if feeding:

        @pl.when(at_end)
        def _():
            pltpu.make_async_copy(send, send, sems.at[0]).wait()


def forward_step(
    tick, chunks, rows, sections, count, place, plan, arrived, inputs, gain, w_in, w_out, kept
):
    width, inner = w_in.shape
    cut = width // count
    shapes = (
        jax.ShapeDtypeStruct((count, rows, cut), BF16),
        pltpu.HBM((count, chunks * rows, cut), BF16),
        pltpu.HBM((chunks * rows, inner + AUX), F32),
        pltpu.HBM((chunks * rows, inner), BF16),
        pltpu.HBM((inner, width), BF16),
        pltpu.HBM((width, inner), BF16),
    )
    specs = [smem(), smem(), vmem(), hbm(), vmem(), vmem(), vmem()] + [hbm()] * len(kept)
    return pl.pallas_call(
        functools.partial(forward_kernel, tick, chunks, sections),
        out_shape=shapes,
        in_specs=specs,
        out_specs=(vmem(),) + (hbm(),) * 5,
        scratch_shapes=[
            pltpu.VMEM((rows, inner + AUX), F32),
            pltpu.VMEM((rows, inner), BF16),
            pltpu.VMEM((2, inner, cut), BF16),
            pltpu.SemaphoreType.DMA((6,)),
        ],
        input_output_aliases={7 + k: 1 + k for k in range(len(kept))},
        compiler_params=pltpu.CompilerParams(vmem_limit_bytes=10 << 20),
        cost_estimate=pl.CostEstimate(
            flops=4 * rows * width * inner, bytes_accessed=10 << 20, transcendentals=0
        ),
        name="forward_step",
    )(
        place,
        plan,
        arrived,
        *kept_in(pltpu.HBM, inputs),
        gain,
        *kept_in(pltpu.VMEM, w_in, w_out),
        *kept_in(pltpu.HBM, *kept),
    )


def giving(chips):
    return {GAP * k: k for k in range(1, chips)}


def receiving(chips):
    return {tick + LATER: k for tick, k in giving(chips).items()}


def backward_kernel(
    tick, chunks, sections, place, arrived, cotangent, x_all, aux_all, hidden_all, gain, w_in, w_out, *rest
):
    chips = x_all.shape[0] // CORES
    tokens = x_all.shape[1]
    got = None
    if tick in receiving(chips):
        got, *rest = rest
    send, late, early, *rest = rest[0 if tick == 0 else 2 :]
    moves = []

    def share(chip, given):
        theirs = x_all.at[pl.ds(chip * CORES, CORES)]
        return [
            pltpu.make_async_copy(theirs, given.at[pl.ds(0, CORES)], rest[-1].at[5]),
            pltpu.make_async_copy(hidden_all, given.at[CORES], rest[-1].at[7]),
        ]

    if tick == 0:
        *rest, own = rest
        for copy in share(place[1], own):
            copy.start()
            copy.wait()
        moves.append(pltpu.make_async_copy(own, early.at[place[1]], rest[-1].at[6]))
    if got is not None:
        source = lax.rem(place[1] + chips - receiving(chips)[tick], chips)
        moves.append(pltpu.make_async_copy(got, early.at[source], rest[-1].at[6]))
    if tick in giving(chips):
        given, *rest = rest
        moves += share(lax.rem(place[1] + giving(chips)[tick], chips), given)
    for move in moves:
        move.start()
    x, aux, grad, sems = rest
    up = arrived
    count, rows, cut = up.shape
    width = count * cut
    inner = w_in.shape[0]
    mine = tick - SKEW * (sections - 1 - place[0])
    active = jnp.logical_and(mine >= 0, mine < chunks)
    at_end = place[0] == 0
    feeding = tick + SKEW < chunks
    if feeding:

        @pl.when(at_end)
        def _():
            for copy in fresh(cotangent, tick + SKEW, None, send, sems.at[0]):
                copy.start()

    @pl.when(active)
    def _():
        at = pl.ds(pl.multiple_of(mine * rows, rows), rows)
        load_x = pltpu.make_async_copy(x_all.at[:, at, :], x, sems.at[1])
        load_x.start()
        load_aux = pltpu.make_async_copy(aux_all.at[at, :], aux, sems.at[2])
        load_aux.start()
        for chip in range(chips):
            theirs = up.at[pl.ds(chip * CORES, CORES)]
            place_of = late.at[chip, pl.ds(0, CORES), at, :]
            pltpu.make_async_copy(theirs, place_of, sems.at[3]).start()

        def project(j, total):
            return total + jnp.dot(up[j], w_out[block(j, cut), :], preferred_element_type=F32)

        grad_hidden = across(count, project, jnp.zeros((rows, inner), F32))
        load_aux.wait()
        pre = aux[:, :inner]
        inverse = aux[:, inner : inner + 1]
        gate = 1.0 / (1.0 + jnp.exp(-pre))
        exact = grad_hidden * gate * (1.0 + pre * (1.0 - gate))
        grad[...] = (exact * inverse).astype(BF16)
        stores = [
            pltpu.make_async_copy(grad, late.at[chip, CORES, at, :], sems.at[4])
            for chip in range(chips)
        ]
        for store in stores:
            store.start()
        grad_pre = exact.astype(BF16)
        mean = jnp.sum(exact * pre, axis=1, keepdims=True) * (inverse / width)
        load_x.wait()

        def expand(j, nothing):
            cols = block(j, cut)
            back = jnp.dot(grad_pre, w_in[:, cols], preferred_element_type=F32)
            inside = back * gain[:, cols] - x[j].astype(F32) * mean
            send[j] = (up[j].astype(F32) + inverse * inside).astype(BF16)
            return nothing

        @pl.when(jnp.logical_not(at_end))
        def _():
            across(count, expand, 0)

        pltpu.make_async_copy(up, up, sems.at[3]).wait()
        written = late.at[:, CORES, pl.ds(0, rows), :]
        pltpu.make_async_copy(written, written, sems.at[4]).wait()

    if feeding:

        @pl.when(at_end)
        def _():
            pltpu.make_async_copy(send, send, sems.at[0]).wait()

    for move in moves:
        move.wait()


def backward_step(
    tick, chunks, rows, sections, place, arrived, cotangent, x_all, aux_all, hidden_all, gain, w_in, w_out, got, kept
):
    inner, width = w_in.shape
    count = x_all.shape[0]
    cut = width // count
    shapes = (
        jax.ShapeDtypeStruct((count, rows, cut), BF16),
        pltpu.HBM((count // CORES, CORES + 1, chunks * rows, cut), BF16),
        pltpu.HBM((count // CORES, CORES + 1, chunks * rows, cut), BF16),
    )
    given = (vmem(),) if tick in giving(count // CORES) else ()
    piece = (CORES + 1, chunks * rows, cut)
    shapes += (jax.ShapeDtypeStruct(piece, BF16),) * len(given)
    specs = [smem(), vmem()] + [hbm()] * 4 + [vmem()] * (3 + len(got)) + [hbm()] * len(kept)
    return pl.pallas_call(
        functools.partial(backward_kernel, tick, chunks, sections),
        out_shape=shapes,
        in_specs=specs,
        out_specs=(vmem(), hbm(), hbm()) + given,
        scratch_shapes=[
            pltpu.VMEM((count, rows, cut), BF16),
            pltpu.VMEM((rows, inner + AUX), F32),
            pltpu.VMEM((rows, inner), BF16),
            pltpu.SemaphoreType.DMA((8,)),
        ]
        + [pltpu.VMEM(piece, BF16)] * (tick == 0),
        input_output_aliases={9 + len(got) + k: 1 + k for k in range(len(kept))},
        compiler_params=pltpu.CompilerParams(vmem_limit_bytes=10 << 20),
        cost_estimate=pl.CostEstimate(
            flops=4 * rows * width * inner, bytes_accessed=10 << 20, transcendentals=0
        ),
        name="backward_step",
    )(
        place,
        arrived,
        *kept_in(pltpu.HBM, cotangent, x_all, aux_all, hidden_all),
        gain,
        *kept_in(pltpu.VMEM, w_in, w_out),
        *got,
        *kept_in(pltpu.HBM, *kept),
    )


def gradient_kernel(place, early, late, own, other, total_in, total_out):
    step = pl.program_id(0)

    @pl.when(step == 0)
    def _():
        total_in[...] = jnp.zeros_like(total_in)
        total_out[...] = jnp.zeros_like(total_out)

    rows = (((0,), (0,)), ((), ()))
    for k in range(TAKEN):
        for core in range(CORES):
            total_in[core] += lax.dot_general(
                early[k, core], late[k, CORES], rows, preferred_element_type=F32
            )
            total_out[core] += lax.dot_general(
                early[k, CORES], late[k, core], rows, preferred_element_type=F32
            )

    @pl.when(step == pl.num_programs(0) - 1)
    def _():
        core = place[2]
        own[0] = total_in[core]
        own[1] = total_out[core]
        other[0] = total_in[1 - core].astype(BF16)
        other[1] = total_out[1 - core].astype(BF16)


def gradients(place, early, late):
    chips, kinds, tokens, cut = early.shape
    block = pl.BlockSpec((TAKEN, kinds, tokens, cut), lambda q: (q, 0, 0, 0))
    result = pl.BlockSpec((2, cut, cut), lambda q: (0, 0, 0))
    return pl.pallas_call(
        gradient_kernel,
        grid=(chips // TAKEN,),
        out_shape=(
            jax.ShapeDtypeStruct((2, cut, cut), F32),
            jax.ShapeDtypeStruct((2, cut, cut), BF16),
        ),
        in_specs=[smem(), block, block],
        out_specs=(result, result),
        scratch_shapes=[pltpu.VMEM((CORES, cut, cut), F32)] * 2,
        compiler_params=pltpu.CompilerParams(vmem_limit_bytes=32 << 20),
        cost_estimate=pl.CostEstimate(
            flops=8 * chips * tokens * cut * cut, bytes_accessed=14 << 20, transcendentals=0
        ),
        name="gradients",
    )(place, *kept_in(pltpu.HBM, early, late))


def per_device(inputs, cotangent, plan_order, norm_gain, weight_in, weight_out):
    sections = lax.axis_size("pipe")
    count = lax.axis_size("dp")
    micro_count, row_count, width = inputs.shape
    chunks = CHUNKS
    rows = micro_count * row_count // chunks
    cut = width // count
    last = SKEW * (sections - 1)
    ticks = chunks + last
    onward = [(s, (s + 1) % sections) for s in range(sections)]
    back = [(after, s) for s, after in onward]
    owner = lax.axis_index("dp")
    chips = count // CORES
    place = [lax.axis_index("pipe"), owner // CORES, owner % CORES]
    place = jnp.stack(place).astype(jnp.int32)
    same_core = [list(range(core, count, CORES)) for core in range(CORES)]
    plan = plan_order.astype(jnp.int32)

    w_in, w_out, early = begin(plan, weight_in[0], weight_out[0], inputs, count, rows)
    moving = dict(enumerate(early))
    kept = ()
    for tick in range(ticks):
        arrived = moving.pop(tick)
        send, *kept = forward_step(
            tick,
            chunks,
            rows,
            sections,
            count,
            place,
            plan,
            arrived,
            inputs,
            norm_gain,
            w_in,
            w_out,
            kept,
        )
        if tick + SKEW < ticks:
            moving[tick + SKEW] = lax.ppermute(send, "pipe", onward)
    x_all, aux_all, hidden_all, w_in_t, w_out_t = kept

    order = jnp.arange(micro_count, dtype=jnp.int32)
    w_in, w_out, early = begin(order, w_in_t, w_out_t, cotangent, count, rows)
    moving = dict(enumerate(early))
    kept = ()
    passing = {}
    for tick in range(ticks):
        arrived = moving.pop(tick)
        got = [passing.pop(tick)] if tick in passing else []
        send, *outs = backward_step(
            tick,
            chunks,
            rows,
            sections,
            place,
            arrived,
            cotangent,
            x_all,
            aux_all,
            hidden_all,
            norm_gain,
            w_in,
            w_out,
            got,
            kept,
        )
        kept, give = outs[:2], outs[2:]
        if tick + SKEW < ticks:
            moving[tick + SKEW] = lax.ppermute(send, "pipe", back)
        if give:
            on = CORES * giving(chips)[tick]
            pairs = [(q, (q + on) % count) for q in range(count)]
            passing[tick + LATER] = lax.ppermute(give[0], "dp", pairs)
    late, early = kept
    late = lax.all_to_all(late, "dp", 0, 0, axis_index_groups=same_core, tiled=True)
    own, other = gradients(place, early, late)
    swapped = [(q, q + 1 if q % CORES == 0 else q - 1) for q in range(count)]
    total = own + lax.ppermute(other, "dp", swapped).astype(F32)
    gain = lax.dynamic_slice(norm_gain[0], (owner * cut,), (cut,))
    grad_in = (total[0] * gain[:, None]).astype(BF16)
    return grad_in[None], total[1].astype(BF16)[None]


def solution(mesh):
    in_specs = (
        P(None, "dp", None),
        P(None, "dp", None),
        P(),
        P("pipe", None),
        P("pipe", None, None),
        P("pipe", None, None),
    )
    out_specs = (P("pipe", "dp", None), P("pipe", None, "dp"))
    return jax.shard_map(
        per_device, mesh=mesh, in_specs=in_specs, out_specs=out_specs, check_vma=False
    )
```

```python
import functools

import jax
import jax.numpy as jnp
from jax import lax
from jax.experimental import pallas as pl
from jax.experimental.pallas import tpu as pltpu
from jax.sharding import PartitionSpec as P

EPSILON = 1e-05
CHUNKS = 12
TAKEN = 2
LOW_FROM = 18
HIGH_FROM = 15
LATER = 4
CORES = 2
SKEW = 2
AUX = 128
TOGETHER = 8

F32 = jnp.float32
BF16 = jnp.bfloat16


def hbm():
    return pl.BlockSpec(memory_space=pltpu.HBM)


def vmem():
    return pl.BlockSpec(memory_space=pltpu.VMEM)


def smem():
    return pl.BlockSpec(memory_space=pltpu.SMEM)


def across(count, body, start):
    def step(j, carry):
        for k in range(TOGETHER):
            carry = body(j * TOGETHER + k, carry)
        return carry

    return lax.fori_loop(0, count // TOGETHER, step, start)


def kept_in(space, *arrays):
    return [pltpu.with_memory_space_constraint(a, space) for a in arrays]


def spread(source, target, at, sem):
    count, _, cut = target.shape
    size = source.shape[0]
    return [
        pltpu.make_async_copy(
            source.at[:, pl.ds(j * cut, cut)], target.at[j, pl.ds(at, size), :], sem
        )
        for j in range(count)
    ]


def pieces(chunk, rows, slot_rows):
    found = []
    row = chunk * rows
    while row < (chunk + 1) * rows:
        slot, offset = divmod(row, slot_rows)
        size = min(slot_rows - offset, (chunk + 1) * rows - row)
        found.append((slot, offset, row - chunk * rows, size))
        row += size
    return found


def fresh(array, chunk, plan, target, sem):
    rows = target.shape[1]
    copies = []
    for slot, offset, at, size in pieces(chunk, rows, array.shape[1]):
        place = plan[slot] if plan is not None else slot
        copies += spread(array.at[place, pl.ds(offset, size), :], target, at, sem)
    return copies


def begin_kernel(plan, first, second, array, first_out, second_out, *rest):
    sems = rest[-1]
    copies = [
        pltpu.make_async_copy(first, first_out, sems.at[0]),
        pltpu.make_async_copy(second, second_out, sems.at[1]),
    ]
    for copy in copies:
        copy.start()
    for chunk, target in enumerate(rest[:-1]):
        for copy in fresh(array, chunk, plan, target, sems.at[2 + chunk]):
            copy.start()
        pltpu.make_async_copy(target, target, sems.at[2 + chunk]).wait()
    for copy in copies:
        copy.wait()


def begin(plan, first, second, array, count, rows):
    chunk = jax.ShapeDtypeStruct((count, rows, array.shape[-1] // count), array.dtype)
    first_out, second_out, *chunks = pl.pallas_call(
        begin_kernel,
        out_shape=(
            pltpu.VMEM(first.shape, first.dtype),
            pltpu.VMEM(second.shape, second.dtype),
        )
        + (chunk,) * SKEW,
        in_specs=[smem()] + [hbm()] * 3,
        out_specs=(vmem(),) * (2 + SKEW),
        scratch_shapes=[pltpu.SemaphoreType.DMA((2 + SKEW,))],
        compiler_params=pltpu.CompilerParams(vmem_limit_bytes=3 << 20),
        name="begin",
    )(plan, *kept_in(pltpu.HBM, first, second, array))
    return first_out, second_out, chunks


def block(j, cut):
    return pl.ds(pl.multiple_of(j * cut, cut), cut)


def giving(chips, ticks):
    low = {LOW_FROM + k - 1: k for k in range(1, chips)}
    high = {ticks + HIGH_FROM + k - 1: k for k in range(1, chips)}
    return low | high


def exchange(now, ticks, sections, place, x_all, hidden_all, early, given, got, sems):
    chips = x_all.shape[0] // CORES
    plan = giving(chips, ticks)
    low = place[0] < sections // 2
    parts = []
    if given is not None:
        chip = lax.rem(place[1] + plan[now], chips)
        theirs = x_all.at[pl.ds(chip * CORES, CORES)]
        taking = low if now < ticks else jnp.logical_not(low)
        parts.append(
            (
                taking,
                [
                    pltpu.make_async_copy(theirs, given.at[pl.ds(0, CORES)], sems.at[0]),
                    pltpu.make_async_copy(hidden_all, given.at[CORES], sems.at[1]),
                ],
            )
        )
    if got is not None:
        source = lax.rem(place[1] + chips - plan[now - LATER], chips)
        taking = low if now - LATER < ticks else jnp.logical_not(low)
        parts.append((taking, [pltpu.make_async_copy(got, early.at[source], sems.at[2])]))
    return parts


def begun(parts):
    for taking, copies in parts:

        @pl.when(taking)
        def _():
            for copy in copies:
                copy.start()


def ended(parts):
    for taking, copies in parts:

        @pl.when(taking)
        def _():
            for copy in copies:
                copy.wait()


def forward_kernel(
    tick, chunks, sections, place, plan, arrived, inputs, gain, w_in, w_out, *rest
):
    ticks = chunks + SKEW * (sections - 1)
    chips = arrived.shape[0] // CORES
    plan_of = giving(chips, ticks)
    got = given = None
    if tick - LATER in plan_of:
        got, *rest = rest
    if tick > 0:
        rest = rest[6:]
    send, x_all, aux_all, hidden_all, w_in_t, w_out_t, early, *rest = rest
    if tick in plan_of:
        given, *rest = rest
    aux, hidden, turned, sems, share_sems = rest
    parts = exchange(
        tick, ticks, sections, place, x_all, hidden_all, early, given, got, share_sems
    )
    begun(parts)
    x = arrived
    count, rows, cut = x.shape
    width = count * cut
    inner = w_in.shape[1]
    mine = tick - SKEW * place[0]
    active = jnp.logical_and(mine >= 0, mine < chunks)

    at_end = place[0] == sections - 1
    feeding = tick + SKEW < chunks
    if feeding:

        @pl.when(at_end)
        def _():
            for copy in fresh(inputs, tick + SKEW, plan, send, sems.at[0]):
                copy.start()

    @pl.when(active)
    def _():
        at = pl.ds(pl.multiple_of(mine * rows, rows), rows)
        store_x = pltpu.make_async_copy(x, x_all.at[:, at, :], sems.at[1])
        store_x.start()

        def project(j, carry):
            total, pre = carry
            value = x[j].astype(F32)
            piece = (value * gain[:, block(j, cut)]).astype(BF16)
            product = jnp.dot(piece, w_in[block(j, cut), :], preferred_element_type=F32)
            return total + value * value, pre + product

        start = jnp.zeros((rows, cut), F32), jnp.zeros((rows, inner), F32)
        total, pre = across(count, project, start)
        inverse = lax.rsqrt(jnp.sum(total, axis=1, keepdims=True) / width + EPSILON)
        pre = pre * inverse
        aux[:, :inner] = pre
        aux[:, inner:] = jnp.broadcast_to(inverse, (rows, AUX))
        store_aux = pltpu.make_async_copy(aux, aux_all.at[at, :], sems.at[2])
        store_aux.start()
        act = (pre / (1.0 + jnp.exp(-pre))).astype(BF16)
        hidden[...] = act
        store_hidden = pltpu.make_async_copy(hidden, hidden_all.at[at, :], sems.at[3])
        store_hidden.start()

        def expand(j, nothing):
            delta = jnp.dot(act, w_out[:, block(j, cut)], preferred_element_type=F32)
            send[j] = (x[j].astype(F32) + delta).astype(BF16)
            return nothing

        @pl.when(jnp.logical_not(at_end))
        def _():
            across(count, expand, 0)

        store_x.wait()
        store_aux.wait()
        store_hidden.wait()

    idle = SKEW * (sections - 1)

    def turn(j):
        turned[0] = w_in[block(j, cut), :].T
        first = pltpu.make_async_copy(turned.at[0], w_in_t.at[:, block(j, cut)], sems.at[4])
        first.start()
        turned[1] = w_out[:, block(j, cut)].T
        second = pltpu.make_async_copy(turned.at[1], w_out_t.at[block(j, cut), :], sems.at[5])
        second.start()
        first.wait()
        second.wait()

    spare = jnp.where(mine < 0, tick, tick - chunks)
    for again in range(-(-count // idle)):
        j = spare + again * idle

        @pl.when(jnp.logical_and(jnp.logical_not(active), j < count))
        def _():
            turn(j)

    if feeding:

        @pl.when(at_end)
        def _():
            pltpu.make_async_copy(send, send, sems.at[0]).wait()

    ended(parts)


def forward_step(
    tick, chunks, rows, sections, count, place, plan, arrived, inputs, gain, w_in, w_out, got, kept
):
    width, inner = w_in.shape
    cut = width // count
    piece = (CORES + 1, chunks * rows, cut)
    sends = tick in giving(count // CORES, chunks + SKEW * (sections - 1))
    shapes = (
        jax.ShapeDtypeStruct((count, rows, cut), BF16),
        pltpu.HBM((count, chunks * rows, cut), BF16),
        pltpu.HBM((chunks * rows, inner + AUX), F32),
        pltpu.HBM((chunks * rows, inner), BF16),
        pltpu.HBM((inner, width), BF16),
        pltpu.HBM((width, inner), BF16),
        pltpu.HBM((count // CORES,) + piece, BF16),
    )
    shapes += (jax.ShapeDtypeStruct(piece, BF16),) * sends
    specs = [smem(), smem(), vmem(), hbm(), vmem(), vmem(), vmem()]
    specs += [vmem()] * len(got) + [hbm()] * len(kept)
    return pl.pallas_call(
        functools.partial(forward_kernel, tick, chunks, sections),
        out_shape=shapes,
        in_specs=specs,
        out_specs=(vmem(),) + (hbm(),) * 6 + (vmem(),) * sends,
        scratch_shapes=[
            pltpu.VMEM((rows, inner + AUX), F32),
            pltpu.VMEM((rows, inner), BF16),
            pltpu.VMEM((2, inner, cut), BF16),
            pltpu.SemaphoreType.DMA((6,)),
            pltpu.SemaphoreType.DMA((3,)),
        ],
        input_output_aliases={7 + len(got) + k: 1 + k for k in range(len(kept))},
        compiler_params=pltpu.CompilerParams(vmem_limit_bytes=12 << 20),
        cost_estimate=pl.CostEstimate(
            flops=4 * rows * width * inner, bytes_accessed=10 << 20, transcendentals=0
        ),
        name="forward_step",
    )(
        place,
        plan,
        arrived,
        *kept_in(pltpu.HBM, inputs),
        gain,
        *kept_in(pltpu.VMEM, w_in, w_out),
        *got,
        *kept_in(pltpu.HBM, *kept),
    )


def backward_kernel(
    tick, chunks, sections, place, arrived, cotangent, x_all, aux_all, hidden_all, gain, w_in, w_out, *rest
):
    ticks = chunks + SKEW * (sections - 1)
    now = ticks + tick
    chips = x_all.shape[0] // CORES
    plan_of = giving(chips, ticks)
    got = given = None
    if now - LATER in plan_of:
        got, *rest = rest
    send, late, early, *rest = rest[1 if tick == 0 else 2 :]
    if now in plan_of:
        given, *rest = rest
    if tick == 0:
        *rest, own = rest
    *rest, share_sems = rest
    parts = exchange(
        now, ticks, sections, place, x_all, hidden_all, early, given, got, share_sems
    )
    begun(parts)
    if tick == 0:
        theirs = x_all.at[pl.ds(place[1] * CORES, CORES)]
        first = pltpu.make_async_copy(theirs, own.at[pl.ds(0, CORES)], rest[-1].at[5])
        second = pltpu.make_async_copy(hidden_all, own.at[CORES], rest[-1].at[6])
        first.start()
        second.start()
        first.wait()
        second.wait()
        third = pltpu.make_async_copy(own, early.at[place[1]], rest[-1].at[5])
        third.start()
    x, aux, grad, sems = rest
    up = arrived
    count, rows, cut = up.shape
    width = count * cut
    inner = w_in.shape[0]
    mine = tick - SKEW * (sections - 1 - place[0])
    active = jnp.logical_and(mine >= 0, mine < chunks)
    at_end = place[0] == 0
    feeding = tick + SKEW < chunks
    if feeding:

        @pl.when(at_end)
        def _():
            for copy in fresh(cotangent, tick + SKEW, None, send, sems.at[0]):
                copy.start()

    @pl.when(active)
    def _():
        at = pl.ds(pl.multiple_of(mine * rows, rows), rows)
        load_x = pltpu.make_async_copy(x_all.at[:, at, :], x, sems.at[1])
        load_x.start()
        load_aux = pltpu.make_async_copy(aux_all.at[at, :], aux, sems.at[2])
        load_aux.start()
        for chip in range(chips):
            theirs = up.at[pl.ds(chip * CORES, CORES)]
            place_of = late.at[chip, pl.ds(0, CORES), at, :]
            pltpu.make_async_copy(theirs, place_of, sems.at[3]).start()

        def project(j, total):
            return total + jnp.dot(up[j], w_out[block(j, cut), :], preferred_element_type=F32)

        grad_hidden = across(count, project, jnp.zeros((rows, inner), F32))
        load_aux.wait()
        pre = aux[:, :inner]
        inverse = aux[:, inner : inner + 1]
        gate = 1.0 / (1.0 + jnp.exp(-pre))
        exact = grad_hidden * gate * (1.0 + pre * (1.0 - gate))
        grad[...] = (exact * inverse).astype(BF16)
        stores = [
            pltpu.make_async_copy(grad, late.at[chip, CORES, at, :], sems.at[4])
            for chip in range(chips)
        ]
        for store in stores:
            store.start()
        grad_pre = exact.astype(BF16)
        mean = jnp.sum(exact * pre, axis=1, keepdims=True) * (inverse / width)
        load_x.wait()

        def expand(j, nothing):
            cols = block(j, cut)
            back = jnp.dot(grad_pre, w_in[:, cols], preferred_element_type=F32)
            inside = back * gain[:, cols] - x[j].astype(F32) * mean
            send[j] = (up[j].astype(F32) + inverse * inside).astype(BF16)
            return nothing

        @pl.when(jnp.logical_not(at_end))
        def _():
            across(count, expand, 0)

        pltpu.make_async_copy(up, up, sems.at[3]).wait()
        written = late.at[:, CORES, pl.ds(0, rows), :]
        pltpu.make_async_copy(written, written, sems.at[4]).wait()

    if feeding:

        @pl.when(at_end)
        def _():
            pltpu.make_async_copy(send, send, sems.at[0]).wait()

    ended(parts)
    if tick == 0:
        third.wait()


def backward_step(
    tick, chunks, rows, sections, place, arrived, cotangent, x_all, aux_all, hidden_all, gain, w_in, w_out, got, kept
):
    inner, width = w_in.shape
    count = x_all.shape[0]
    cut = width // count
    shapes = (
        jax.ShapeDtypeStruct((count, rows, cut), BF16),
        pltpu.HBM((count // CORES, CORES + 1, chunks * rows, cut), BF16),
        pltpu.HBM((count // CORES, CORES + 1, chunks * rows, cut), BF16),
    )
    ticks = chunks + SKEW * (sections - 1)
    given = (vmem(),) if ticks + tick in giving(count // CORES, ticks) else ()
    piece = (CORES + 1, chunks * rows, cut)
    shapes += (jax.ShapeDtypeStruct(piece, BF16),) * len(given)
    specs = [smem(), vmem()] + [hbm()] * 4 + [vmem()] * (3 + len(got)) + [hbm()] * len(kept)
    return pl.pallas_call(
        functools.partial(backward_kernel, tick, chunks, sections),
        out_shape=shapes,
        in_specs=specs,
        out_specs=(vmem(), hbm(), hbm()) + given,
        scratch_shapes=[
            pltpu.VMEM((count, rows, cut), BF16),
            pltpu.VMEM((rows, inner + AUX), F32),
            pltpu.VMEM((rows, inner), BF16),
            pltpu.SemaphoreType.DMA((7,)),
            pltpu.SemaphoreType.DMA((3,)),
        ]
        + [pltpu.VMEM(piece, BF16)] * (tick == 0),
        input_output_aliases={9 + len(got) + k: 3 - len(kept) + k for k in range(len(kept))},
        compiler_params=pltpu.CompilerParams(vmem_limit_bytes=10 << 20),
        cost_estimate=pl.CostEstimate(
            flops=4 * rows * width * inner, bytes_accessed=10 << 20, transcendentals=0
        ),
        name="backward_step",
    )(
        place,
        arrived,
        *kept_in(pltpu.HBM, cotangent, x_all, aux_all, hidden_all),
        gain,
        *kept_in(pltpu.VMEM, w_in, w_out),
        *got,
        *kept_in(pltpu.HBM, *kept),
    )


def gradient_kernel(place, early, late, own, other, total_in, total_out):
    step = pl.program_id(0)

    @pl.when(step == 0)
    def _():
        total_in[...] = jnp.zeros_like(total_in)
        total_out[...] = jnp.zeros_like(total_out)

    rows = (((0,), (0,)), ((), ()))
    for k in range(TAKEN):
        for core in range(CORES):
            total_in[core] += lax.dot_general(
                early[k, core], late[k, CORES], rows, preferred_element_type=F32
            )
            total_out[core] += lax.dot_general(
                early[k, CORES], late[k, core], rows, preferred_element_type=F32
            )

    @pl.when(step == pl.num_programs(0) - 1)
    def _():
        core = place[2]
        own[0] = total_in[core]
        own[1] = total_out[core]
        other[0] = total_in[1 - core].astype(BF16)
        other[1] = total_out[1 - core].astype(BF16)


def gradients(place, early, late):
    chips, kinds, tokens, cut = early.shape
    block = pl.BlockSpec((TAKEN, kinds, tokens, cut), lambda q: (q, 0, 0, 0))
    result = pl.BlockSpec((2, cut, cut), lambda q: (0, 0, 0))
    return pl.pallas_call(
        gradient_kernel,
        grid=(chips // TAKEN,),
        out_shape=(
            jax.ShapeDtypeStruct((2, cut, cut), F32),
            jax.ShapeDtypeStruct((2, cut, cut), BF16),
        ),
        in_specs=[smem(), block, block],
        out_specs=(result, result),
        scratch_shapes=[pltpu.VMEM((CORES, cut, cut), F32)] * 2,
        compiler_params=pltpu.CompilerParams(vmem_limit_bytes=32 << 20),
        cost_estimate=pl.CostEstimate(
            flops=8 * chips * tokens * cut * cut, bytes_accessed=14 << 20, transcendentals=0
        ),
        name="gradients",
    )(place, *kept_in(pltpu.HBM, early, late))


def per_device(inputs, cotangent, plan_order, norm_gain, weight_in, weight_out):
    sections = lax.axis_size("pipe")
    count = lax.axis_size("dp")
    micro_count, row_count, width = inputs.shape
    chunks = CHUNKS
    rows = micro_count * row_count // chunks
    cut = width // count
    last = SKEW * (sections - 1)
    ticks = chunks + last
    onward = [(s, (s + 1) % sections) for s in range(sections)]
    back = [(after, s) for s, after in onward]
    owner = lax.axis_index("dp")
    chips = count // CORES
    place = [lax.axis_index("pipe"), owner // CORES, owner % CORES]
    place = jnp.stack(place).astype(jnp.int32)
    same_core = [list(range(core, count, CORES)) for core in range(CORES)]
    plan = plan_order.astype(jnp.int32)

    w_in, w_out, early = begin(plan, weight_in[0], weight_out[0], inputs, count, rows)
    moving = dict(enumerate(early))
    half = sections // 2
    plan_of = giving(chips, ticks)
    passing = {}

    def pass_on(block, now):
        first = 0 if now < ticks else half
        on = CORES * plan_of[now]
        pairs = [
            (s * count + q, s * count + (q + on) % count)
            for s in range(first, first + half)
            for q in range(count)
        ]
        passing[now + LATER] = lax.ppermute(block, ("pipe", "dp"), pairs)

    kept = ()
    for tick in range(ticks):
        arrived = moving.pop(tick)
        got = [passing.pop(tick)] if tick in passing else []
        send, *outs = forward_step(
            tick,
            chunks,
            rows,
            sections,
            count,
            place,
            plan,
            arrived,
            inputs,
            norm_gain,
            w_in,
            w_out,
            got,
            kept,
        )
        kept, give = outs[:6], outs[6:]
        if tick + SKEW < ticks:
            moving[tick + SKEW] = lax.ppermute(send, "pipe", onward)
        if give:
            pass_on(give[0], tick)
    x_all, aux_all, hidden_all, w_in_t, w_out_t, exchanged = kept

    order = jnp.arange(micro_count, dtype=jnp.int32)
    w_in, w_out, early = begin(order, w_in_t, w_out_t, cotangent, count, rows)
    moving = dict(enumerate(early))
    kept = [exchanged]
    for tick in range(ticks):
        arrived = moving.pop(tick)
        got = [passing.pop(ticks + tick)] if ticks + tick in passing else []
        send, *outs = backward_step(
            tick,
            chunks,
            rows,
            sections,
            place,
            arrived,
            cotangent,
            x_all,
            aux_all,
            hidden_all,
            norm_gain,
            w_in,
            w_out,
            got,
            kept,
        )
        kept, give = outs[:2], outs[2:]
        if tick + SKEW < ticks:
            moving[tick + SKEW] = lax.ppermute(send, "pipe", back)
        if give:
            pass_on(give[0], ticks + tick)
    late, early = kept
    late = lax.all_to_all(late, "dp", 0, 0, axis_index_groups=same_core, tiled=True)
    own, other = gradients(place, early, late)
    swapped = [(q, q + 1 if q % CORES == 0 else q - 1) for q in range(count)]
    total = own + lax.ppermute(other, "dp", swapped).astype(F32)
    gain = lax.dynamic_slice(norm_gain[0], (owner * cut,), (cut,))
    grad_in = (total[0] * gain[:, None]).astype(BF16)
    return grad_in[None], total[1].astype(BF16)[None]


def solution(mesh):
    in_specs = (
        P(None, "dp", None),
        P(None, "dp", None),
        P(),
        P("pipe", None),
        P("pipe", None, None),
        P("pipe", None, None),
    )
    out_specs = (P("pipe", "dp", None), P("pipe", None, "dp"))
    return jax.shard_map(
        per_device, mesh=mesh, in_specs=in_specs, out_specs=out_specs, check_vma=False
    )
```

```python
import functools

import jax
import jax.numpy as jnp
from jax import lax
from jax.experimental import pallas as pl
from jax.experimental.pallas import tpu as pltpu
from jax.sharding import PartitionSpec as P

EPSILON = 1e-05
CHUNKS = 12
TAKEN = 2
CORES = 2
SKEW = 2
AUX = 128
TOGETHER = 8

ROWS_X, ROWS_UP, ROWS_HIDDEN, ROWS_GRAD, KINDS = 0, 2, 4, 5, 6

F32 = jnp.float32
BF16 = jnp.bfloat16


def hbm():
    return pl.BlockSpec(memory_space=pltpu.HBM)


def vmem():
    return pl.BlockSpec(memory_space=pltpu.VMEM)


def smem():
    return pl.BlockSpec(memory_space=pltpu.SMEM)


def across(count, body, start):
    def step(j, carry):
        for k in range(TOGETHER):
            carry = body(j * TOGETHER + k, carry)
        return carry

    return lax.fori_loop(0, count // TOGETHER, step, start)


def kept_in(space, *arrays):
    return [pltpu.with_memory_space_constraint(a, space) for a in arrays]


def spread(source, target, at, sem):
    count, _, cut = target.shape
    size = source.shape[0]
    return [
        pltpu.make_async_copy(
            source.at[:, pl.ds(j * cut, cut)], target.at[j, pl.ds(at, size), :], sem
        )
        for j in range(count)
    ]


def pieces(chunk, rows, slot_rows):
    found = []
    row = chunk * rows
    while row < (chunk + 1) * rows:
        slot, offset = divmod(row, slot_rows)
        size = min(slot_rows - offset, (chunk + 1) * rows - row)
        found.append((slot, offset, row - chunk * rows, size))
        row += size
    return found


def fresh(array, chunk, plan, target, sem):
    rows = target.shape[1]
    copies = []
    for slot, offset, at, size in pieces(chunk, rows, array.shape[1]):
        place = plan[slot] if plan is not None else slot
        copies += spread(array.at[place, pl.ds(offset, size), :], target, at, sem)
    return copies


def begin_kernel(plan, first, second, array, first_out, second_out, *rest):
    sems = rest[-1]
    copies = [
        pltpu.make_async_copy(first, first_out, sems.at[0]),
        pltpu.make_async_copy(second, second_out, sems.at[1]),
    ]
    for copy in copies:
        copy.start()
    for chunk, target in enumerate(rest[:-1]):
        for copy in fresh(array, chunk, plan, target, sems.at[2 + chunk]):
            copy.start()
        pltpu.make_async_copy(target, target, sems.at[2 + chunk]).wait()
    for copy in copies:
        copy.wait()


def begin(plan, first, second, array, count, rows):
    chunk = jax.ShapeDtypeStruct((count, rows, array.shape[-1] // count), array.dtype)
    first_out, second_out, *chunks = pl.pallas_call(
        begin_kernel,
        out_shape=(
            pltpu.VMEM(first.shape, first.dtype),
            pltpu.VMEM(second.shape, second.dtype),
        )
        + (chunk,) * SKEW,
        in_specs=[smem()] + [hbm()] * 3,
        out_specs=(vmem(),) * (2 + SKEW),
        scratch_shapes=[pltpu.SemaphoreType.DMA((2 + SKEW,))],
        compiler_params=pltpu.CompilerParams(vmem_limit_bytes=3 << 20),
        name="begin",
    )(plan, *kept_in(pltpu.HBM, first, second, array))
    return first_out, second_out, chunks


def block(j, cut):
    return pl.ds(pl.multiple_of(j * cut, cut), cut)


def by_chip(block, shared, at, kind, sem):
    return [
        pltpu.make_async_copy(
            block.at[pl.ds(chip * CORES, CORES)],
            shared.at[chip, pl.ds(kind, CORES), at, :],
            sem,
        )
        for chip in range(shared.shape[0])
    ]


def for_all(rows, shared, at, kind, sem):
    return [
        pltpu.make_async_copy(rows, shared.at[chip, kind, at, :], sem)
        for chip in range(shared.shape[0])
    ]


def forward_kernel(
    tick, chunks, sections, place, plan, arrived, inputs, gain, w_in, w_out, *rest
):
    if tick > 0:
        rest = rest[4:]
    send, shared, aux_all, w_in_t, w_out_t, *rest = rest
    aux, hidden, turned, sems = rest
    x = arrived
    count, rows, cut = x.shape
    width = count * cut
    inner = w_in.shape[1]
    mine = tick - SKEW * place[0]
    active = jnp.logical_and(mine >= 0, mine < chunks)

    at_end = place[0] == sections - 1
    feeding = tick + SKEW < chunks
    if feeding:

        @pl.when(at_end)
        def _():
            for copy in fresh(inputs, tick + SKEW, plan, send, sems.at[0]):
                copy.start()

    @pl.when(active)
    def _():
        at = pl.ds(pl.multiple_of(mine * rows, rows), rows)
        for copy in by_chip(x, shared, at, ROWS_X, sems.at[1]):
            copy.start()

        def project(j, carry):
            total, pre = carry
            value = x[j].astype(F32)
            piece = (value * gain[:, block(j, cut)]).astype(BF16)
            product = jnp.dot(piece, w_in[block(j, cut), :], preferred_element_type=F32)
            return total + value * value, pre + product

        start = jnp.zeros((rows, cut), F32), jnp.zeros((rows, inner), F32)
        total, pre = across(count, project, start)
        inverse = lax.rsqrt(jnp.sum(total, axis=1, keepdims=True) / width + EPSILON)
        pre = pre * inverse
        aux[:, :inner] = pre
        aux[:, inner:] = jnp.broadcast_to(inverse, (rows, AUX))
        store_aux = pltpu.make_async_copy(aux, aux_all.at[at, :], sems.at[2])
        store_aux.start()
        act = (pre / (1.0 + jnp.exp(-pre))).astype(BF16)
        hidden[...] = act
        for copy in for_all(hidden, shared, at, ROWS_HIDDEN, sems.at[3]):
            copy.start()

        def expand(j, nothing):
            delta = jnp.dot(act, w_out[:, block(j, cut)], preferred_element_type=F32)
            send[j] = (x[j].astype(F32) + delta).astype(BF16)
            return nothing

        @pl.when(jnp.logical_not(at_end))
        def _():
            across(count, expand, 0)

        pltpu.make_async_copy(x, x, sems.at[1]).wait()
        store_aux.wait()
        written = shared.at[:, ROWS_HIDDEN, pl.ds(0, rows), :]
        pltpu.make_async_copy(written, written, sems.at[3]).wait()

    idle = SKEW * (sections - 1)

    def turn(j):
        turned[0] = w_in[block(j, cut), :].T
        first = pltpu.make_async_copy(turned.at[0], w_in_t.at[:, block(j, cut)], sems.at[4])
        first.start()
        turned[1] = w_out[:, block(j, cut)].T
        second = pltpu.make_async_copy(turned.at[1], w_out_t.at[block(j, cut), :], sems.at[5])
        second.start()
        first.wait()
        second.wait()

    spare = jnp.where(mine < 0, tick, tick - chunks)
    for again in range(-(-count // idle)):
        j = spare + again * idle

        @pl.when(jnp.logical_and(jnp.logical_not(active), j < count))
        def _():
            turn(j)

    if feeding:

        @pl.when(at_end)
        def _():
            pltpu.make_async_copy(send, send, sems.at[0]).wait()


def forward_step(
    tick, chunks, rows, sections, count, place, plan, arrived, inputs, gain, w_in, w_out, kept
):
    width, inner = w_in.shape
    cut = width // count
    shapes = (
        jax.ShapeDtypeStruct((count, rows, cut), BF16),
        pltpu.HBM((count // CORES, KINDS, chunks * rows, cut), BF16),
        pltpu.HBM((chunks * rows, inner + AUX), F32),
        pltpu.HBM((inner, width), BF16),
        pltpu.HBM((width, inner), BF16),
    )
    specs = [smem(), smem(), vmem(), hbm(), vmem(), vmem(), vmem()] + [hbm()] * len(kept)
    return pl.pallas_call(
        functools.partial(forward_kernel, tick, chunks, sections),
        out_shape=shapes,
        in_specs=specs,
        out_specs=(vmem(),) + (hbm(),) * 4,
        scratch_shapes=[
            pltpu.VMEM((rows, inner + AUX), F32),
            pltpu.VMEM((rows, inner), BF16),
            pltpu.VMEM((2, inner, cut), BF16),
            pltpu.SemaphoreType.DMA((6,)),
        ],
        input_output_aliases={7 + k: 1 + k for k in range(len(kept))},
        compiler_params=pltpu.CompilerParams(vmem_limit_bytes=10 << 20),
        cost_estimate=pl.CostEstimate(
            flops=4 * rows * width * inner, bytes_accessed=10 << 20, transcendentals=0
        ),
        name="forward_step",
    )(
        place,
        plan,
        arrived,
        *kept_in(pltpu.HBM, inputs),
        gain,
        *kept_in(pltpu.VMEM, w_in, w_out),
        *kept_in(pltpu.HBM, *kept),
    )


def backward_kernel(
    tick, chunks, sections, place, arrived, cotangent, aux_all, gain, w_in, w_out, *rest
):
    send, shared, x, aux, grad, sems = rest[1:]
    up = arrived
    count, rows, cut = up.shape
    width = count * cut
    inner = w_in.shape[0]
    mine = tick - SKEW * (sections - 1 - place[0])
    active = jnp.logical_and(mine >= 0, mine < chunks)
    at_end = place[0] == 0
    feeding = tick + SKEW < chunks
    if feeding:

        @pl.when(at_end)
        def _():
            for copy in fresh(cotangent, tick + SKEW, None, send, sems.at[0]):
                copy.start()

    @pl.when(active)
    def _():
        at = pl.ds(pl.multiple_of(mine * rows, rows), rows)
        for chip in range(shared.shape[0]):
            theirs = shared.at[chip, pl.ds(ROWS_X, CORES), at, :]
            here = x.at[pl.ds(chip * CORES, CORES)]
            pltpu.make_async_copy(theirs, here, sems.at[1]).start()
        load_aux = pltpu.make_async_copy(aux_all.at[at, :], aux, sems.at[2])
        load_aux.start()
        for copy in by_chip(up, shared, at, ROWS_UP, sems.at[3]):
            copy.start()

        def project(j, total):
            return total + jnp.dot(up[j], w_out[block(j, cut), :], preferred_element_type=F32)

        grad_hidden = across(count, project, jnp.zeros((rows, inner), F32))
        load_aux.wait()
        pre = aux[:, :inner]
        inverse = aux[:, inner : inner + 1]
        gate = 1.0 / (1.0 + jnp.exp(-pre))
        exact = grad_hidden * gate * (1.0 + pre * (1.0 - gate))
        grad[...] = (exact * inverse).astype(BF16)
        for copy in for_all(grad, shared, at, ROWS_GRAD, sems.at[4]):
            copy.start()
        grad_pre = exact.astype(BF16)
        mean = jnp.sum(exact * pre, axis=1, keepdims=True) * (inverse / width)
        pltpu.make_async_copy(x, x, sems.at[1]).wait()

        def expand(j, nothing):
            cols = block(j, cut)
            back = jnp.dot(grad_pre, w_in[:, cols], preferred_element_type=F32)
            inside = back * gain[:, cols] - x[j].astype(F32) * mean
            send[j] = (up[j].astype(F32) + inverse * inside).astype(BF16)
            return nothing

        @pl.when(jnp.logical_not(at_end))
        def _():
            across(count, expand, 0)

        pltpu.make_async_copy(up, up, sems.at[3]).wait()
        written = shared.at[:, ROWS_GRAD, pl.ds(0, rows), :]
        pltpu.make_async_copy(written, written, sems.at[4]).wait()

    if feeding:

        @pl.when(at_end)
        def _():
            pltpu.make_async_copy(send, send, sems.at[0]).wait()


def backward_step(
    tick, chunks, rows, sections, place, arrived, cotangent, aux_all, gain, w_in, w_out, shared
):
    inner, width = w_in.shape
    count, rows, cut = arrived.shape
    return pl.pallas_call(
        functools.partial(backward_kernel, tick, chunks, sections),
        out_shape=(
            jax.ShapeDtypeStruct((count, rows, cut), BF16),
            pltpu.HBM(shared.shape, BF16),
        ),
        in_specs=[smem(), vmem(), hbm(), hbm(), vmem(), vmem(), vmem(), hbm()],
        out_specs=(vmem(), hbm()),
        scratch_shapes=[
            pltpu.VMEM((count, rows, cut), BF16),
            pltpu.VMEM((rows, inner + AUX), F32),
            pltpu.VMEM((rows, inner), BF16),
            pltpu.SemaphoreType.DMA((5,)),
        ],
        input_output_aliases={7: 1},
        compiler_params=pltpu.CompilerParams(vmem_limit_bytes=10 << 20),
        cost_estimate=pl.CostEstimate(
            flops=4 * rows * width * inner, bytes_accessed=10 << 20, transcendentals=0
        ),
        name="backward_step",
    )(
        place,
        arrived,
        *kept_in(pltpu.HBM, cotangent, aux_all),
        gain,
        *kept_in(pltpu.VMEM, w_in, w_out),
        *kept_in(pltpu.HBM, shared),
    )


def gradient_kernel(place, taken, own, other, total_in, total_out):
    step = pl.program_id(0)

    @pl.when(step == 0)
    def _():
        total_in[...] = jnp.zeros_like(total_in)
        total_out[...] = jnp.zeros_like(total_out)

    rows = (((0,), (0,)), ((), ()))
    for k in range(TAKEN):
        for core in range(CORES):
            total_in[core] += lax.dot_general(
                taken[k, ROWS_X + core], taken[k, ROWS_GRAD], rows, preferred_element_type=F32
            )
            total_out[core] += lax.dot_general(
                taken[k, ROWS_HIDDEN], taken[k, ROWS_UP + core], rows, preferred_element_type=F32
            )

    @pl.when(step == pl.num_programs(0) - 1)
    def _():
        core = place[2]
        own[0] = total_in[core]
        own[1] = total_out[core]
        other[0] = total_in[1 - core].astype(BF16)
        other[1] = total_out[1 - core].astype(BF16)


def gradients(place, taken):
    chips, kinds, tokens, cut = taken.shape
    block = pl.BlockSpec((TAKEN, kinds, tokens, cut), lambda q: (q, 0, 0, 0))
    result = pl.BlockSpec((2, cut, cut), lambda q: (0, 0, 0))
    return pl.pallas_call(
        gradient_kernel,
        grid=(chips // TAKEN,),
        out_shape=(
            jax.ShapeDtypeStruct((2, cut, cut), F32),
            jax.ShapeDtypeStruct((2, cut, cut), BF16),
        ),
        in_specs=[smem(), block],
        out_specs=(result, result),
        scratch_shapes=[pltpu.VMEM((CORES, cut, cut), F32)] * 2,
        compiler_params=pltpu.CompilerParams(vmem_limit_bytes=32 << 20),
        cost_estimate=pl.CostEstimate(
            flops=8 * chips * tokens * cut * cut, bytes_accessed=14 << 20, transcendentals=0
        ),
        name="gradients",
    )(place, *kept_in(pltpu.HBM, taken))


def per_device(inputs, cotangent, plan_order, norm_gain, weight_in, weight_out):
    sections = lax.axis_size("pipe")
    count = lax.axis_size("dp")
    micro_count, row_count, width = inputs.shape
    chunks = CHUNKS
    rows = micro_count * row_count // chunks
    cut = width // count
    last = SKEW * (sections - 1)
    ticks = chunks + last
    onward = [(s, (s + 1) % sections) for s in range(sections)]
    back = [(after, s) for s, after in onward]
    owner = lax.axis_index("dp")
    place = [lax.axis_index("pipe"), owner // CORES, owner % CORES]
    place = jnp.stack(place).astype(jnp.int32)
    same_core = [list(range(core, count, CORES)) for core in range(CORES)]
    plan = plan_order.astype(jnp.int32)

    w_in, w_out, early = begin(plan, weight_in[0], weight_out[0], inputs, count, rows)
    moving = dict(enumerate(early))
    kept = ()
    for tick in range(ticks):
        arrived = moving.pop(tick)
        send, *kept = forward_step(
            tick,
            chunks,
            rows,
            sections,
            count,
            place,
            plan,
            arrived,
            inputs,
            norm_gain,
            w_in,
            w_out,
            kept,
        )
        if tick + SKEW < ticks:
            moving[tick + SKEW] = lax.ppermute(send, "pipe", onward)
    shared, aux_all, w_in_t, w_out_t = kept

    order = jnp.arange(micro_count, dtype=jnp.int32)
    w_in, w_out, early = begin(order, w_in_t, w_out_t, cotangent, count, rows)
    moving = dict(enumerate(early))
    for tick in range(ticks):
        arrived = moving.pop(tick)
        send, shared = backward_step(
            tick,
            chunks,
            rows,
            sections,
            place,
            arrived,
            cotangent,
            aux_all,
            norm_gain,
            w_in,
            w_out,
            shared,
        )
        if tick + SKEW < ticks:
            moving[tick + SKEW] = lax.ppermute(send, "pipe", back)
    taken = lax.all_to_all(shared, "dp", 0, 0, axis_index_groups=same_core, tiled=True)
    own, other = gradients(place, taken)
    swapped = [(q, q + 1 if q % CORES == 0 else q - 1) for q in range(count)]
    total = own + lax.ppermute(other, "dp", swapped).astype(F32)
    gain = lax.dynamic_slice(norm_gain[0], (owner * cut,), (cut,))
    grad_in = (total[0] * gain[:, None]).astype(BF16)
    return grad_in[None], total[1].astype(BF16)[None]


def solution(mesh):
    in_specs = (
        P(None, "dp", None),
        P(None, "dp", None),
        P(),
        P("pipe", None),
        P("pipe", None, None),
        P("pipe", None, None),
    )
    out_specs = (P("pipe", "dp", None), P("pipe", None, "dp"))
    return jax.shard_map(
        per_device, mesh=mesh, in_specs=in_specs, out_specs=out_specs, check_vma=False
    )
```

```python
import functools

import jax
import jax.numpy as jnp
from jax import lax
from jax.experimental import pallas as pl
from jax.experimental.pallas import tpu as pltpu
from jax.sharding import PartitionSpec as P

EPSILON = 1e-05
CHUNKS = 12
TAKEN = 2
CORES = 2
SKEW = 2
AUX = 128
TOGETHER = 8

ROWS_X, ROWS_UP, ROWS_HIDDEN, KINDS = 0, 2, 4, 5

F32 = jnp.float32
BF16 = jnp.bfloat16


def hbm():
    return pl.BlockSpec(memory_space=pltpu.HBM)


def vmem():
    return pl.BlockSpec(memory_space=pltpu.VMEM)


def smem():
    return pl.BlockSpec(memory_space=pltpu.SMEM)


def across(count, body, start):
    def step(j, carry):
        for k in range(TOGETHER):
            carry = body(j * TOGETHER + k, carry)
        return carry

    return lax.fori_loop(0, count // TOGETHER, step, start)


def kept_in(space, *arrays):
    return [pltpu.with_memory_space_constraint(a, space) for a in arrays]


def spread(source, target, at, sem):
    count, _, cut = target.shape
    size = source.shape[0]
    return [
        pltpu.make_async_copy(
            source.at[:, pl.ds(j * cut, cut)], target.at[j, pl.ds(at, size), :], sem
        )
        for j in range(count)
    ]


def pieces(chunk, rows, slot_rows):
    found = []
    row = chunk * rows
    while row < (chunk + 1) * rows:
        slot, offset = divmod(row, slot_rows)
        size = min(slot_rows - offset, (chunk + 1) * rows - row)
        found.append((slot, offset, row - chunk * rows, size))
        row += size
    return found


def fresh(array, chunk, plan, target, sem):
    rows = target.shape[1]
    copies = []
    for slot, offset, at, size in pieces(chunk, rows, array.shape[1]):
        place = plan[slot] if plan is not None else slot
        copies += spread(array.at[place, pl.ds(offset, size), :], target, at, sem)
    return copies


def begin_kernel(plan, first, second, array, first_out, second_out, *rest):
    sems = rest[-1]
    copies = [
        pltpu.make_async_copy(first, first_out, sems.at[0]),
        pltpu.make_async_copy(second, second_out, sems.at[1]),
    ]
    for copy in copies:
        copy.start()
    for chunk, target in enumerate(rest[:-1]):
        for copy in fresh(array, chunk, plan, target, sems.at[2 + chunk]):
            copy.start()
        pltpu.make_async_copy(target, target, sems.at[2 + chunk]).wait()
    for copy in copies:
        copy.wait()


def begin(plan, first, second, array, count, rows):
    chunk = jax.ShapeDtypeStruct((count, rows, array.shape[-1] // count), array.dtype)
    first_out, second_out, *chunks = pl.pallas_call(
        begin_kernel,
        out_shape=(
            pltpu.VMEM(first.shape, first.dtype),
            pltpu.VMEM(second.shape, second.dtype),
        )
        + (chunk,) * SKEW,
        in_specs=[smem()] + [hbm()] * 3,
        out_specs=(vmem(),) * (2 + SKEW),
        scratch_shapes=[pltpu.SemaphoreType.DMA((2 + SKEW,))],
        compiler_params=pltpu.CompilerParams(vmem_limit_bytes=3 << 20),
        name="begin",
    )(plan, *kept_in(pltpu.HBM, first, second, array))
    return first_out, second_out, chunks


def block(j, cut):
    return pl.ds(pl.multiple_of(j * cut, cut), cut)


def by_chip(block, shared, at, kind, sem):
    return [
        pltpu.make_async_copy(
            block.at[pl.ds(chip * CORES, CORES)],
            shared.at[chip, pl.ds(kind, CORES), at, :],
            sem,
        )
        for chip in range(shared.shape[0])
    ]


def for_all(rows, shared, at, kind, sem):
    return [
        pltpu.make_async_copy(rows, shared.at[chip, kind, at, :], sem)
        for chip in range(shared.shape[0])
    ]


def forward_kernel(
    tick, chunks, sections, place, plan, arrived, inputs, gain, w_in, w_out, *rest
):
    if tick > 0:
        rest = rest[4:]
    send, shared, aux_all, w_in_t, w_out_t, *rest = rest
    aux, hidden, turned, sems = rest
    x = arrived
    count, rows, cut = x.shape
    width = count * cut
    inner = w_in.shape[1]
    mine = tick - SKEW * place[0]
    active = jnp.logical_and(mine >= 0, mine < chunks)

    at_end = place[0] == sections - 1
    feeding = tick + SKEW < chunks
    if feeding:

        @pl.when(at_end)
        def _():
            for copy in fresh(inputs, tick + SKEW, plan, send, sems.at[0]):
                copy.start()

    @pl.when(active)
    def _():
        at = pl.ds(pl.multiple_of(mine * rows, rows), rows)
        for copy in by_chip(x, shared, at, ROWS_X, sems.at[1]):
            copy.start()

        def project(j, carry):
            total, pre = carry
            value = x[j].astype(F32)
            piece = (value * gain[:, block(j, cut)]).astype(BF16)
            product = jnp.dot(piece, w_in[block(j, cut), :], preferred_element_type=F32)
            return total + value * value, pre + product

        start = jnp.zeros((rows, cut), F32), jnp.zeros((rows, inner), F32)
        total, pre = across(count, project, start)
        inverse = lax.rsqrt(jnp.sum(total, axis=1, keepdims=True) / width + EPSILON)
        pre = pre * inverse
        aux[:, :inner] = pre
        aux[:, inner:] = jnp.broadcast_to(inverse, (rows, AUX))
        store_aux = pltpu.make_async_copy(aux, aux_all.at[at, :], sems.at[2])
        store_aux.start()
        act = (pre / (1.0 + jnp.exp(-pre))).astype(BF16)
        hidden[...] = act
        for copy in for_all(hidden, shared, at, ROWS_HIDDEN, sems.at[3]):
            copy.start()

        def expand(j, nothing):
            delta = jnp.dot(act, w_out[:, block(j, cut)], preferred_element_type=F32)
            send[j] = (x[j].astype(F32) + delta).astype(BF16)
            return nothing

        @pl.when(jnp.logical_not(at_end))
        def _():
            across(count, expand, 0)

        pltpu.make_async_copy(x, x, sems.at[1]).wait()
        store_aux.wait()
        written = shared.at[:, ROWS_HIDDEN, pl.ds(0, rows), :]
        pltpu.make_async_copy(written, written, sems.at[3]).wait()

    idle = SKEW * (sections - 1)

    def turn(j):
        turned[0] = w_in[block(j, cut), :].T
        first = pltpu.make_async_copy(turned.at[0], w_in_t.at[:, block(j, cut)], sems.at[4])
        first.start()
        turned[1] = w_out[:, block(j, cut)].T
        second = pltpu.make_async_copy(turned.at[1], w_out_t.at[block(j, cut), :], sems.at[5])
        second.start()
        first.wait()
        second.wait()

    spare = jnp.where(mine < 0, tick, tick - chunks)
    for again in range(-(-count // idle)):
        j = spare + again * idle

        @pl.when(jnp.logical_and(jnp.logical_not(active), j < count))
        def _():
            turn(j)

    if feeding:

        @pl.when(at_end)
        def _():
            pltpu.make_async_copy(send, send, sems.at[0]).wait()


def forward_step(
    tick, chunks, rows, sections, count, place, plan, arrived, inputs, gain, w_in, w_out, kept
):
    width, inner = w_in.shape
    cut = width // count
    shapes = (
        jax.ShapeDtypeStruct((count, rows, cut), BF16),
        pltpu.HBM((count // CORES, KINDS, chunks * rows, cut), BF16),
        pltpu.HBM((chunks * rows, inner + AUX), F32),
        pltpu.HBM((inner, width), BF16),
        pltpu.HBM((width, inner), BF16),
    )
    specs = [smem(), smem(), vmem(), hbm(), vmem(), vmem(), vmem()] + [hbm()] * len(kept)
    return pl.pallas_call(
        functools.partial(forward_kernel, tick, chunks, sections),
        out_shape=shapes,
        in_specs=specs,
        out_specs=(vmem(),) + (hbm(),) * 4,
        scratch_shapes=[
            pltpu.VMEM((rows, inner + AUX), F32),
            pltpu.VMEM((rows, inner), BF16),
            pltpu.VMEM((2, inner, cut), BF16),
            pltpu.SemaphoreType.DMA((6,)),
        ],
        input_output_aliases={7 + k: 1 + k for k in range(len(kept))},
        compiler_params=pltpu.CompilerParams(vmem_limit_bytes=10 << 20),
        cost_estimate=pl.CostEstimate(
            flops=4 * rows * width * inner, bytes_accessed=10 << 20, transcendentals=0
        ),
        name="forward_step",
    )(
        place,
        plan,
        arrived,
        *kept_in(pltpu.HBM, inputs),
        gain,
        *kept_in(pltpu.VMEM, w_in, w_out),
        *kept_in(pltpu.HBM, *kept),
    )


def backward_kernel(
    tick, chunks, sections, place, arrived, cotangent, aux_all, gain, w_in, w_out, *rest
):
    send, shared, grad_all, x, aux, grad, sems = rest[1 if tick == 0 else 2 :]
    up = arrived
    count, rows, cut = up.shape
    width = count * cut
    inner = w_in.shape[0]
    mine = tick - SKEW * (sections - 1 - place[0])
    active = jnp.logical_and(mine >= 0, mine < chunks)
    at_end = place[0] == 0
    feeding = tick + SKEW < chunks
    if feeding:

        @pl.when(at_end)
        def _():
            for copy in fresh(cotangent, tick + SKEW, None, send, sems.at[0]):
                copy.start()

    @pl.when(active)
    def _():
        at = pl.ds(pl.multiple_of(mine * rows, rows), rows)
        for chip in range(shared.shape[0]):
            theirs = shared.at[chip, pl.ds(ROWS_X, CORES), at, :]
            here = x.at[pl.ds(chip * CORES, CORES)]
            pltpu.make_async_copy(theirs, here, sems.at[1]).start()
        load_aux = pltpu.make_async_copy(aux_all.at[at, :], aux, sems.at[2])
        load_aux.start()
        for copy in by_chip(up, shared, at, ROWS_UP, sems.at[3]):
            copy.start()

        def project(j, total):
            return total + jnp.dot(up[j], w_out[block(j, cut), :], preferred_element_type=F32)

        grad_hidden = across(count, project, jnp.zeros((rows, inner), F32))
        load_aux.wait()
        pre = aux[:, :inner]
        inverse = aux[:, inner : inner + 1]
        gate = 1.0 / (1.0 + jnp.exp(-pre))
        exact = grad_hidden * gate * (1.0 + pre * (1.0 - gate))
        grad[...] = (exact * inverse).astype(BF16)
        store_grad = pltpu.make_async_copy(grad, grad_all.at[at, :], sems.at[4])
        store_grad.start()
        grad_pre = exact.astype(BF16)
        mean = jnp.sum(exact * pre, axis=1, keepdims=True) * (inverse / width)
        pltpu.make_async_copy(x, x, sems.at[1]).wait()

        def expand(j, nothing):
            cols = block(j, cut)
            back = jnp.dot(grad_pre, w_in[:, cols], preferred_element_type=F32)
            inside = back * gain[:, cols] - x[j].astype(F32) * mean
            send[j] = (up[j].astype(F32) + inverse * inside).astype(BF16)
            return nothing

        @pl.when(jnp.logical_not(at_end))
        def _():
            across(count, expand, 0)

        pltpu.make_async_copy(up, up, sems.at[3]).wait()
        store_grad.wait()

    if feeding:

        @pl.when(at_end)
        def _():
            pltpu.make_async_copy(send, send, sems.at[0]).wait()


def backward_step(
    tick, chunks, rows, sections, place, arrived, cotangent, aux_all, gain, w_in, w_out, kept
):
    inner, width = w_in.shape
    count, rows, cut = arrived.shape
    return pl.pallas_call(
        functools.partial(backward_kernel, tick, chunks, sections),
        out_shape=(
            jax.ShapeDtypeStruct((count, rows, cut), BF16),
            pltpu.HBM(kept[0].shape, BF16),
            pltpu.HBM((chunks * rows, inner), BF16),
        ),
        in_specs=[smem(), vmem(), hbm(), hbm(), vmem(), vmem(), vmem()] + [hbm()] * len(kept),
        out_specs=(vmem(), hbm(), hbm()),
        scratch_shapes=[
            pltpu.VMEM((count, rows, cut), BF16),
            pltpu.VMEM((rows, inner + AUX), F32),
            pltpu.VMEM((rows, inner), BF16),
            pltpu.SemaphoreType.DMA((5,)),
        ],
        input_output_aliases={7 + k: 1 + k for k in range(len(kept))},
        compiler_params=pltpu.CompilerParams(vmem_limit_bytes=10 << 20),
        cost_estimate=pl.CostEstimate(
            flops=4 * rows * width * inner, bytes_accessed=10 << 20, transcendentals=0
        ),
        name="backward_step",
    )(
        place,
        arrived,
        *kept_in(pltpu.HBM, cotangent, aux_all),
        gain,
        *kept_in(pltpu.VMEM, w_in, w_out),
        *kept_in(pltpu.HBM, *kept),
    )


def gradient_kernel(place, taken, grad, own, other, total_in, total_out):
    step = pl.program_id(0)

    @pl.when(step == 0)
    def _():
        total_in[...] = jnp.zeros_like(total_in)
        total_out[...] = jnp.zeros_like(total_out)

    rows = (((0,), (0,)), ((), ()))
    for k in range(TAKEN):
        for core in range(CORES):
            total_in[core] += lax.dot_general(
                taken[k, ROWS_X + core], grad[k], rows, preferred_element_type=F32
            )
            total_out[core] += lax.dot_general(
                taken[k, ROWS_HIDDEN], taken[k, ROWS_UP + core], rows, preferred_element_type=F32
            )

    @pl.when(step == pl.num_programs(0) - 1)
    def _():
        core = place[2]
        own[0] = total_in[core]
        own[1] = total_out[core]
        other[0] = total_in[1 - core].astype(BF16)
        other[1] = total_out[1 - core].astype(BF16)


def gradients(place, taken, grad):
    chips, kinds, tokens, cut = taken.shape
    block = pl.BlockSpec((TAKEN, kinds, tokens, cut), lambda q: (q, 0, 0, 0))
    inner = pl.BlockSpec((TAKEN, tokens, cut), lambda q: (q, 0, 0))
    result = pl.BlockSpec((2, cut, cut), lambda q: (0, 0, 0))
    return pl.pallas_call(
        gradient_kernel,
        grid=(chips // TAKEN,),
        out_shape=(
            jax.ShapeDtypeStruct((2, cut, cut), F32),
            jax.ShapeDtypeStruct((2, cut, cut), BF16),
        ),
        in_specs=[smem(), block, inner],
        out_specs=(result, result),
        scratch_shapes=[pltpu.VMEM((CORES, cut, cut), F32)] * 2,
        compiler_params=pltpu.CompilerParams(vmem_limit_bytes=32 << 20),
        cost_estimate=pl.CostEstimate(
            flops=8 * chips * tokens * cut * cut, bytes_accessed=14 << 20, transcendentals=0
        ),
        name="gradients",
    )(place, *kept_in(pltpu.HBM, taken, grad))


def per_device(inputs, cotangent, plan_order, norm_gain, weight_in, weight_out):
    sections = lax.axis_size("pipe")
    count = lax.axis_size("dp")
    micro_count, row_count, width = inputs.shape
    chunks = CHUNKS
    rows = micro_count * row_count // chunks
    cut = width // count
    last = SKEW * (sections - 1)
    ticks = chunks + last
    onward = [(s, (s + 1) % sections) for s in range(sections)]
    back = [(after, s) for s, after in onward]
    owner = lax.axis_index("dp")
    place = [lax.axis_index("pipe"), owner // CORES, owner % CORES]
    place = jnp.stack(place).astype(jnp.int32)
    same_core = [list(range(core, count, CORES)) for core in range(CORES)]
    plan = plan_order.astype(jnp.int32)

    w_in, w_out, early = begin(plan, weight_in[0], weight_out[0], inputs, count, rows)
    moving = dict(enumerate(early))
    kept = ()
    for tick in range(ticks):
        arrived = moving.pop(tick)
        send, *kept = forward_step(
            tick,
            chunks,
            rows,
            sections,
            count,
            place,
            plan,
            arrived,
            inputs,
            norm_gain,
            w_in,
            w_out,
            kept,
        )
        if tick + SKEW < ticks:
            moving[tick + SKEW] = lax.ppermute(send, "pipe", onward)
    shared, aux_all, w_in_t, w_out_t = kept
    kept = [shared]

    order = jnp.arange(micro_count, dtype=jnp.int32)
    w_in, w_out, early = begin(order, w_in_t, w_out_t, cotangent, count, rows)
    moving = dict(enumerate(early))
    for tick in range(ticks):
        arrived = moving.pop(tick)
        send, *kept = backward_step(
            tick,
            chunks,
            rows,
            sections,
            place,
            arrived,
            cotangent,
            aux_all,
            norm_gain,
            w_in,
            w_out,
            kept,
        )
        if tick + SKEW < ticks:
            moving[tick + SKEW] = lax.ppermute(send, "pipe", back)
    shared, grad_all = kept
    grad_rows = lax.all_gather(grad_all, "dp", axis_index_groups=same_core)
    taken = lax.all_to_all(shared, "dp", 0, 0, axis_index_groups=same_core, tiled=True)
    own, other = gradients(place, taken, grad_rows)
    swapped = [(q, q + 1 if q % CORES == 0 else q - 1) for q in range(count)]
    total = own + lax.ppermute(other, "dp", swapped).astype(F32)
    gain = lax.dynamic_slice(norm_gain[0], (owner * cut,), (cut,))
    grad_in = (total[0] * gain[:, None]).astype(BF16)
    return grad_in[None], total[1].astype(BF16)[None]


def solution(mesh):
    in_specs = (
        P(None, "dp", None),
        P(None, "dp", None),
        P(),
        P("pipe", None),
        P("pipe", None, None),
        P("pipe", None, None),
    )
    out_specs = (P("pipe", "dp", None), P("pipe", None, "dp"))
    return jax.shard_map(
        per_device, mesh=mesh, in_specs=in_specs, out_specs=out_specs, check_vma=False
    )
```
